128 devices in a mesh: shot: 8 (over z, core), bin: 16 (over y, x).
Axes of the slice: x: 4, y: 4, z: 4, core: 2. Of those that a mesh axis runs over, the one named last changes fastest.
Arguments:
- traces: bfloat16 [32768, 2048], P(('shot', 'bin')), may hold values from -6 to 6
- shot_filter: bfloat16 [128, 128], P(('shot', 'bin')), may hold values from -0.5 to 0.5
- channel_gain: float32 [256], replicated, may hold values from 0.5 to 2
- bin_owner: int32 [32768, 1], P(('shot', 'bin')), may hold values from 0 to 127; in each aligned block of 256 rows (0 to 255, 256 to 511, ...) at most 4 rows name the same one
- bin_slot: int32 [32768], P(('shot', 'bin')), may hold values from 0 to 15
- offset_class: int32 [32768], P(('shot', 'bin')), may hold values from 0 to 31
- dip_filter: bfloat16 [9, 31], replicated, may hold values from -0.375 to 0.375
- nmo_start: int32 [32, 2048], replicated, may hold values from 0 to 2040, as said below
- nmo_weights: bfloat16 [32, 8, 2048], replicated, may hold values from -2.09375 to 2.09375
Outputs:
- stacked: float32 [16, 128, 2048], P('shot', 'bin')
The draws below stay inside these ranges and needn't reach their ends.
Inputs may be any that keep to these rules, and one draw needn't show every extreme that they name: `bin_owner`: among the rows of one device, at most 4 name any one block. `nmo_start`: band starts leave room for all 8 taps and lie at most 64 samples before their output sample.
All inputs are finite; a program needn't handle non-finite values.
Results may differ from the reference program's by a relative error of at most 0.0042.
Values may be sent and summed in bfloat16 or wider, within the bound.
No kernel may reach another device: no remote copies, remote signals or barrier semaphores. Data moves between devices by JAX's collectives and lax.ppermute only.
A program may use at most 256 MiB of HBM per device.

```python
import math
import jax
import jax.numpy as jnp
import numpy as np
from jax import lax

NT = 2048
DECON_TAPS = 128
DIP_XL = 9
DIP_T = 31
NMO_TAPS = 8
NOFF = 32
CHANNELS = 256
IL_DEV = 2
XL_DEV = 8
OWNERS = 128
TR_DEV = 256
TRACES = 32768
SHOTS = 128
CAP = 4
BINS_DEV = 16
NIL = 16
NXL = 128
N_BIN = 16


def draw_nmo_start(key, part):
    delays = jax.random.randint(key, (NOFF, NT), 0, 64)
    sample_times = jnp.arange(NT, dtype=jnp.int32)[None, :]
    return jnp.clip(sample_times + delays - 64, 0, NT - NMO_TAPS).astype(jnp.int32)


def plant(result, stream_key, low, largest):
    dims = result.shape
    index_at = [jax.random.randint(jax.random.fold_in(stream_key, axis), (), 0, dims[axis]) for axis in range(len(dims))]
    result = result.at[tuple(index_at)].set(low)
    longest = dims.index(max(dims))
    index_at[longest] = (index_at[longest] + 1) % dims[longest]
    return result.at[tuple(index_at)].set(largest)


def level_of(own_key, extent, pieces, smallest, high):
    def one(axis_at, parts):
        heights = jax.random.uniform(jax.random.fold_in(jax.random.fold_in(own_key, 6), axis_at), (parts,), jnp.float32, smallest / len(pieces), high / len(pieces))
        return jnp.repeat(jnp.exp(heights), extent[axis_at] // parts).reshape((-1,) + (1,) * (len(extent) - axis_at - 1))

    level = one(*pieces[0])
    for cut in pieces[1:]:
        level = level * one(*cut)
    return level


def deal_out(own_key, own, number, rows, number_of, top, most, lean):
    ranking = jax.random.permutation(own_key, number_of)
    crowded, common = shares(number_of, rows * top, most, lean, True), shares(number_of, rows * top, most, lean, False)
    places = jnp.arange(number_of)

    def named(sizes, offset_by):
        used = int((sizes > 0).sum())
        fixed = max(1, used // 4)
        shifted = fixed + (places - fixed + offset_by * (used - fixed)) % max(1, number_of - fixed)
        return jnp.zeros((number_of,), jnp.int32).at[ranking[jnp.where(places < fixed, places, shifted)]].set(jnp.asarray(sizes, jnp.int32))

    sizes = jnp.where(number % 4 == 0, named(crowded, number // 4), named(common, number - number // 4 - 1))
    mixed = jax.random.permutation(jax.random.fold_in(own, 3), number_of)
    donor, sink = mixed[0:number_of // 2 * 2:2], mixed[1:number_of // 2 * 2:2]
    slack = jnp.minimum(sizes[donor] - 1, most - sizes[sink]) // 2
    slack = jnp.where((donor == ranking[0]) | (sink == ranking[0]) | (sizes[sink] == 0), 0, jnp.maximum(slack, 0))
    shifted = jax.random.randint(jax.random.fold_in(own, 4), (number_of // 2,), 0, 1 << 20) % (slack + 1)
    sizes = sizes.at[donor].add(-shifted).at[sink].add(shifted)
    items = jnp.searchsorted(jnp.cumsum(sizes), jnp.arange(rows * top), side="right").astype(jnp.int32)
    listing = items.reshape(top, rows).T
    listing = listing[jax.random.permutation(jax.random.fold_in(own, 1), rows)]
    offset_by = jax.random.randint(jax.random.fold_in(own, 2), (rows, 1), 0, top)
    return jnp.take_along_axis(listing, (jnp.arange(top)[None, :] + offset_by) % top, axis=1)


def shares(count, total, reach, slope, full):
    loads = [(1 << 20) // math.isqrt(standing ** slope) + 1 for standing in range(1, count + 1)]
    largest = reach if full else min(reach, max(-(-total // count), total * loads[0] // sum(loads)))
    least = 1 if total - largest >= count - 1 else 0
    holding, rest = [largest] + [least] * (count - 1), total - largest - least * (count - 1)
    while rest > 0:
        candidates = [i for i in range(1, count) if holding[i] < largest] or [i for i in range(1, count) if holding[i] < reach]
        mass, remaining = sum([loads[i] for i in candidates]), rest
        for i in candidates:
            addition = min(reach - holding[i], max(1, remaining * loads[i] // mass), rest)
            holding[i] = holding[i] + addition
            rest = rest - addition
    return np.array(holding)


def scatter_about(rng, extent, deviation, reach, cuts=(), held_as=jnp.bfloat16):
    array = deviation * jax.random.normal(rng, extent, jnp.float32)
    if cuts:
        array = array * level_of(rng, extent, cuts, -0.22, 0.18)
    return jnp.clip(array, -reach, reach).astype(held_as)


def setup_inputs(seed: int = 0) -> dict:
    keys = jax.random.split(jax.random.key(seed), 10)
    traces = scatter_about(keys[0], (TRACES, NT), 1.0, 6.0, ((0, 128),))
    shot_filter = scatter_about(keys[1], (SHOTS, DECON_TAPS), DECON_TAPS ** -0.5, 0.5, ((0, 128),))
    channel_gain = jnp.clip(jnp.exp(jax.random.uniform(keys[2], (CHANNELS,), jnp.float32, math.log(0.5), math.log(2.0))), 0.5, 2.0)
    bin_owner_keys = jax.random.split(jax.random.fold_in(keys[3], 1), TRACES // TR_DEV)
    bin_owner_turns = jax.random.permutation(jax.random.fold_in(keys[3], 3), TRACES // TR_DEV)
    bin_owner = jax.vmap(lambda own, number: deal_out(jax.random.fold_in(keys[3], 2), own, number, TR_DEV, OWNERS, 1, CAP, 2))(bin_owner_keys, bin_owner_turns).reshape((TRACES, 1))
    bin_slot = plant(jax.random.randint(keys[4], (TRACES,), 0, BINS_DEV), jax.random.fold_in(keys[4], 1), 0, BINS_DEV - 1).astype(jnp.int32)
    offset_class = plant(jax.random.randint(keys[5], (TRACES,), 0, NOFF), jax.random.fold_in(keys[5], 1), 0, NOFF - 1).astype(jnp.int32)
    dip_filter = scatter_about(keys[6], (DIP_XL, DIP_T), (DIP_XL * DIP_T) ** -0.5, 0.375)
    nmo_start = draw_nmo_start(jax.random.fold_in(keys[9], 71), 0)
    nmo_weights = scatter_about(keys[8], (NOFF, NMO_TAPS, NT), 0.35, 2.09375)
    return {"traces": traces, "shot_filter": shot_filter, "channel_gain": channel_gain, "bin_owner": bin_owner, "bin_slot": bin_slot, "offset_class": offset_class, "dip_filter": dip_filter, "nmo_start": nmo_start, "nmo_weights": nmo_weights}


def later_block(values):
    pad_zero = jnp.zeros_like(values[..., :1, :])
    return jnp.concatenate((pad_zero, values[..., :-1, :]), axis=-2)

def earlier_block(values):
    pad_zero = jnp.zeros_like(values[..., :1, :])
    return jnp.concatenate((values[..., 1:, :], pad_zero), axis=-2)

def decon_matrices_of(shot_filter):
    row_index = jnp.arange(128, dtype=jnp.int32)[:, None]
    col_index = jnp.arange(256, dtype=jnp.int32)[None, :]
    lag_index = col_index % 128 - row_index - 128 * (col_index // 128 - 1)
    valid = (lag_index >= 0) & (lag_index < 128)
    picked = jnp.take(shot_filter, jnp.clip(lag_index, 0, 127).reshape(-1), axis=1).reshape(shot_filter.shape[0], 128, 256)
    return jnp.where(valid[None], picked, jnp.zeros((), shot_filter.dtype)).astype(jnp.bfloat16)

def dip_matrices_of(dip_filter):
    time_taps = dip_filter.shape[1]
    row_index = jnp.arange(128, dtype=jnp.int32)[:, None]
    col_index = jnp.arange(384, dtype=jnp.int32)[None, :]
    difference = 128 * (col_index // 128 - 1) + row_index - col_index % 128 + time_taps // 2
    valid = (difference >= 0) & (difference < time_taps)
    picked = jnp.take(dip_filter, jnp.clip(difference, 0, time_taps - 1).reshape(-1), axis=1).reshape(dip_filter.shape[0], 128, 384)
    return jnp.where(valid[None], picked, jnp.zeros((), dip_filter.dtype)).astype(jnp.bfloat16)

def dip_sum(padded, matrices, out_width):
    lead = padded.shape[0]
    offsets = padded.shape[2]
    blocks = padded.shape[3] // 128
    block_shape = (lead, out_width, offsets, blocks, 128)
    summed = jnp.zeros(block_shape, jnp.float32)
    for tap_index in range(matrices.shape[0]):
        trace_rows = padded[:, tap_index:tap_index + out_width].reshape(-1, 128)
        before = jnp.dot(trace_rows, matrices[tap_index, :, :128], preferred_element_type=jnp.float32).reshape(block_shape)
        centre = jnp.dot(trace_rows, matrices[tap_index, :, 128:256], preferred_element_type=jnp.float32).reshape(block_shape)
        following = jnp.dot(trace_rows, matrices[tap_index, :, 256:], preferred_element_type=jnp.float32).reshape(block_shape)
        summed = summed + later_block(before) + centre + earlier_block(following)
    return summed

def move_out(filtered, band_start, weights):
    summed = jnp.zeros(filtered.shape, jnp.float32)
    for tap_index in range(weights.shape[1]):
        sample_index = jnp.broadcast_to((band_start + tap_index)[None], filtered.shape)
        picked = jnp.take_along_axis(filtered, sample_index, axis=2).astype(jnp.float32)
        summed = summed + picked * weights[:, tap_index, :].astype(jnp.float32)[None]
    return lax.optimization_barrier(jnp.sum(summed, axis=1)) / math.sqrt(filtered.shape[1])

def reference(traces, shot_filter, channel_gain, bin_owner, bin_slot, offset_class, dip_filter, nmo_start, nmo_weights):
    blocks = NT // 128
    decon_matrices = decon_matrices_of(shot_filter)
    shot_rows = traces.reshape(SHOTS, CHANNELS * blocks, 128)

    def apply_shot(shot_pair):
        trace_rows, matrix = shot_pair
        product = jnp.dot(trace_rows, matrix, preferred_element_type=jnp.float32).reshape(CHANNELS, blocks, 256)
        return later_block(product[:, :, :128]) + product[:, :, 128:]
    convolved = lax.map(apply_shot, (shot_rows, decon_matrices))
    deconvolved = (convolved * channel_gain[None, :, None, None]).astype(jnp.bfloat16).reshape(TRACES, NT)
    owner_index = bin_owner[:, 0]
    inline = owner_index // N_BIN * IL_DEV + bin_slot // XL_DEV
    crossline = owner_index % N_BIN * XL_DEV + bin_slot % XL_DEV
    cell = ((inline * NXL + crossline) * NOFF + offset_class).astype(jnp.int32)
    cell_total = NIL * NXL * NOFF
    summed = jax.ops.segment_sum(deconvolved.astype(jnp.float32), cell, num_segments=cell_total)
    fold_count = jax.ops.segment_sum(jnp.ones((TRACES,), jnp.float32), cell, num_segments=cell_total)
    binned = (summed / jnp.maximum(fold_count, 1.0)[:, None]).astype(jnp.bfloat16).reshape(NIL, NXL, NOFF, NT)
    dip_matrices = dip_matrices_of(dip_filter)
    rim_width = DIP_XL // 2
    padded = jnp.pad(binned, ((0, 0), (rim_width, rim_width), (0, 0), (0, 0)))

    def apply_inline(inline_plane):
        summed_dip = dip_sum(inline_plane[None], dip_matrices, NXL)[0]
        filtered = summed_dip.reshape(NXL, NOFF, NT).astype(jnp.bfloat16)
        return move_out(filtered, nmo_start, nmo_weights)
    return lax.map(apply_inline, padded)
```

```python
import math

import jax
import jax.numpy as jnp
from jax import lax
from jax.experimental import pallas as pl
from jax.experimental.pallas import tpu as pltpu
from jax.sharding import PartitionSpec as P

LANES = 128
IL_DEV = 2
XL_DEV = 8
CAP = 4
HALVES = 2
F32 = jnp.float32
BF16 = jnp.bfloat16


def iota(shape, dim):
    return lax.broadcasted_iota(jnp.int32, shape, dim)


def send_kernel(traces, shot_filter, gain, owner, slot, offset, out, placed, filtered):
    rows, samples = traces.shape
    blocks = samples // LANES
    half = samples // HALVES
    offsets = 32
    slots = slot[...]
    hi = (slots % XL_DEV) * IL_DEV + slots // XL_DEV
    lo = offset[...]
    lane_row = iota((LANES, rows), 0)
    table = jnp.where(lane_row == 0, 1.0, 0.0)
    table = jnp.where(lane_row == 1, jnp.broadcast_to(hi.astype(F32), table.shape), table)
    table = jnp.where(lane_row == 2, jnp.broadcast_to(lo.astype(F32), table.shape), table)
    table = jnp.where(lane_row == 3, jnp.broadcast_to(gain[...], table.shape), table)
    table = jnp.where(lane_row == 4, jnp.broadcast_to(owner[...].astype(F32), table.shape), table)
    columns = table.T
    gain_column = columns[:, 3:4]
    owner_column = columns[:, 4:5].astype(jnp.int32)
    codes = jnp.where(iota(columns.shape, 1) < 3, columns, 0.0).astype(BF16)
    owner_row = owner[...]
    same = (owner_column == owner_row) & (iota((rows, rows), 0) < iota((rows, rows), 1))
    rank = jnp.sum(jnp.where(same, 1.0, 0.0), axis=0, keepdims=True).astype(jnp.int32)
    target = owner_row * (CAP * HALVES) + rank
    out_rows = out.shape[0]
    row_ids = iota((out_rows, rows), 0)
    for h in range(HALVES):
        placed[:, h * rows : (h + 1) * rows] = jnp.where(
            row_ids == target + h * CAP, 1.0, 0.0
        ).astype(BF16)
    taps = jnp.broadcast_to(shot_filter[...].astype(F32), (LANES, LANES))
    circulant = pltpu.roll(taps, 0, 1, stride=1, stride_axis=0)
    later = iota((LANES, LANES), 0) > iota((LANES, LANES), 1)
    before = jnp.where(later, circulant, 0.0).astype(BF16)
    centre = jnp.where(later, 0.0, circulant).astype(BF16)
    matrix = jnp.concatenate([before, centre], axis=0)
    for j in range(blocks):
        if j == 0:
            value = jnp.dot(traces[:, :LANES], centre, preferred_element_type=F32)
        else:
            value = jnp.dot(
                traces[:, (j - 1) * LANES : (j + 1) * LANES], matrix, preferred_element_type=F32
            )
        h, at = divmod(j * LANES, half)
        filtered[h * rows : (h + 1) * rows, at : at + LANES] = (value * gain_column).astype(BF16)
    for h in range(HALVES):
        filtered[h * rows : (h + 1) * rows, half:] = codes
    width = 2 * LANES
    for n in range(0, filtered.shape[1], width):
        stop = min(n + width, filtered.shape[1])
        out[:, n:stop] = jnp.dot(
            placed[...], filtered[:, n:stop], preferred_element_type=F32
        ).astype(BF16)


def stack_kernel(arrived, dip, start, weights, centre, right, left, windows, dips, dipped):
    slots = arrived.shape[0]
    half = arrived.shape[1] - LANES
    offsets, samples = start.shape
    blocks = samples // LANES
    lines = IL_DEV * offsets
    cells = XL_DEV * lines
    taps_x = dip.shape[0]
    rim = XL_DEV // 2
    out_lines = 2 * XL_DEV
    codes = arrived[:, half:]
    rows = codes.astype(F32).T
    code = jnp.where(rows[0:1] > 0.5, rows[1:2] * offsets + rows[2:3], -1.0).astype(jnp.int32)
    part = (iota((1, slots), 1) // CAP) % HALVES
    cell_ids = iota((cells, slots), 0)
    members = []
    for h in range(HALVES):
        hit = cell_ids == jnp.where(part == h, code, -1)
        members.append(jnp.where(hit, 1.0, 0.0).astype(BF16))
    fold = jnp.dot(members[0], codes, preferred_element_type=F32)[:, 0:1]
    scale = 1.0 / jnp.maximum(fold, 1.0)
    zero = jnp.zeros((lines, LANES), BF16)
    for x in range(XL_DEV):
        windows[0, :, 2 * x * LANES : (2 * x + 1) * LANES] = zero
        windows[blocks, :, (2 * x + 1) * LANES : (2 * x + 2) * LANES] = zero
    width = 2 * LANES
    for h in range(HALVES):
        for n in range(0, half, width):
            binned = (
                jnp.dot(members[h], arrived[:, n : n + width], preferred_element_type=F32) * scale
            ).astype(BF16)
            for b in range(width // LANES):
                block = (h * half + n) // LANES + b
                for x in range(XL_DEV):
                    piece = binned[x * lines : (x + 1) * lines, b * LANES : (b + 1) * LANES]
                    windows[block, :, (2 * x + 1) * LANES : (2 * x + 2) * LANES] = piece
                    windows[block + 1, :, 2 * x * LANES : (2 * x + 1) * LANES] = piece
    bands = []
    for a in range(taps_x):
        spread = jnp.broadcast_to(dip[a : a + 1, :], (2 * LANES, 2 * LANES))
        band = pltpu.roll(spread, 0, 1, stride=1, stride_axis=0)
        bands.append(band[:, :LANES].astype(BF16))
    none = jnp.zeros((2 * LANES, LANES), BF16)
    for d in range(taps_x + 1):
        dips[d * width : (d + 1) * width, :LANES] = bands[d] if d < taps_x else none
        dips[d * width : (d + 1) * width, LANES:] = bands[d - 1] if d > 0 else none

    group = dipped.shape[0] // 3

    def filter_group(g, carry):
        first = g * group
        for pair in range(out_lines // 2):
            low = max(0, 2 * pair - 2 * rim)
            high = min(XL_DEV, 2 * pair + 2)
            d = low - 2 * pair + 2 * rim
            lhs = windows[pl.ds(first, group), :, low * width : high * width]
            value = jnp.dot(
                lhs.reshape(group * lines, (high - low) * width),
                dips[d * width : (d + high - low) * width, :],
                preferred_element_type=F32,
            )
            for m in range(group):
                for i in range(IL_DEV):
                    for s in range(2):
                        line = (2 * pair + s - rim) % out_lines
                        at = m * lines + i * offsets
                        dipped[first + m, pl.ds(i * out_lines + line, offsets, stride=2 * out_lines), :] = (
                            value[at : at + offsets, s * LANES : (s + 1) * LANES]
                        )
        return carry

    lax.fori_loop(0, 3, filter_group, 0)

    tile = 8
    groups = 2 * LANES // tile
    span = 2 * out_lines
    sublane = iota((tile, LANES), 0)
    root = 1.0 / math.sqrt(offsets)

    def move_out(j, carry):
        at = pl.multiple_of(j * LANES, LANES)
        firsts = start[:, pl.ds(at, LANES)] + (LANES // 2 - at)
        total = jnp.zeros((span, LANES), F32)
        for o in range(offsets):
            first = jnp.broadcast_to(firsts[o : o + 1, :], (tile, LANES))
            turned = weights[o, :, pl.ds(at, LANES)].astype(F32)
            for bit in (1, 2, 4):
                turned = jnp.where(
                    (first & bit) != 0, pltpu.roll(turned, bit, 0), turned
                )
            place = (first - sublane + (tile - 1)) >> 3
            band = jnp.concatenate(
                [jnp.where(place == g, turned, 0.0) for g in range(groups)], axis=0
            ).astype(BF16)
            rows = pl.ds(o * span, span)
            lhs = jnp.concatenate(
                [dipped[j, rows, :].astype(BF16), dipped[j + 1, rows, :].astype(BF16)], axis=1
            )
            total = total + jnp.dot(lhs, band, preferred_element_type=F32)
        total = total * root
        for i in range(IL_DEV):
            base = i * out_lines
            centre[i, :, pl.ds(at, LANES)] = total[base : base + XL_DEV, :]
            right[i, :, pl.ds(at, LANES)] = total[base + XL_DEV : base + XL_DEV + rim, :]
            left[i, :, pl.ds(at, LANES)] = total[base + XL_DEV + rim : base + out_lines, :]
        return carry

    lax.fori_loop(0, blocks, move_out, 0)


def whole(count):
    return [pl.BlockSpec(memory_space=pltpu.VMEM)] * count


def send_call(traces, shot_filter, channel_gain, bin_owner, bin_slot, offset_class, owners):
    rows, samples = traces.shape
    width = samples // HALVES + LANES
    per_owner = CAP * HALVES
    return pl.pallas_call(
        send_kernel,
        out_shape=jax.ShapeDtypeStruct((owners * per_owner, width), BF16),
        in_specs=whole(6),
        out_specs=pl.BlockSpec(memory_space=pltpu.VMEM),
        scratch_shapes=[
            pltpu.VMEM((owners * per_owner, HALVES * rows), BF16),
            pltpu.VMEM((HALVES * rows, width), BF16),
        ],
    )(
        traces,
        shot_filter,
        channel_gain.reshape(1, rows),
        bin_owner.reshape(1, rows),
        bin_slot.reshape(1, rows),
        offset_class.reshape(1, rows),
    )


def stack_call(arrived, dip_filter, nmo_start, nmo_weights):
    offsets, samples = nmo_start.shape
    taps_x, taps_t = dip_filter.shape
    begin = 2 * LANES - LANES // 2 - taps_t // 2
    spread = jnp.pad(
        dip_filter[:, ::-1].astype(F32), ((0, 0), (begin, 2 * LANES - begin - taps_t))
    )
    steps = 18
    lines = IL_DEV * offsets
    edge = jax.ShapeDtypeStruct((IL_DEV, XL_DEV // 2, samples), F32)
    return pl.pallas_call(
        stack_kernel,
        out_shape=(jax.ShapeDtypeStruct((IL_DEV, XL_DEV, samples), F32), edge, edge),
        in_specs=whole(4),
        out_specs=tuple(whole(3)),
        scratch_shapes=[
            pltpu.VMEM((steps, lines, 2 * LANES * XL_DEV), BF16),
            pltpu.VMEM(((taps_x + 1) * 2 * LANES, 2 * LANES), BF16),
            pltpu.VMEM((steps, 2 * XL_DEV * lines, LANES), F32),
        ],
    )(arrived, spread, nmo_start, nmo_weights)


def per_device(
    traces,
    shot_filter,
    channel_gain,
    bin_owner,
    bin_slot,
    offset_class,
    dip_filter,
    nmo_start,
    nmo_weights,
):
    owners = lax.axis_size("shot") * lax.axis_size("bin")
    outgoing = send_call(
        traces, shot_filter, channel_gain, bin_owner, bin_slot, offset_class, owners
    )
    rows, width = outgoing.shape
    arrived = lax.all_to_all(
        outgoing.reshape(owners, rows // owners, width), ("shot", "bin"), 0, 0, tiled=True
    ).reshape(rows, width)
    centre, right, left = stack_call(arrived, dip_filter, nmo_start, nmo_weights)
    count = lax.axis_size("bin")
    ends = range(count - 1)
    from_left = lax.ppermute(right, "bin", [(i, i + 1) for i in ends])
    from_right = lax.ppermute(left, "bin", [(i + 1, i) for i in ends])
    return centre + jnp.concatenate([from_left, from_right], axis=1)


def solution(mesh):
    placed = (
        P(("shot", "bin"), None),
        P(("shot", "bin"), None),
        P(),
        P(("shot", "bin"), None),
        P(("shot", "bin")),
        P(("shot", "bin")),
        P(),
        P(),
        P(),
    )
    return jax.shard_map(
        per_device, mesh=mesh, in_specs=placed, out_specs=P("shot", "bin", None), check_vma=False
    )
```

```python
import math

import jax
import jax.numpy as jnp
from jax import lax
from jax.experimental import pallas as pl
from jax.experimental.pallas import tpu as pltpu
from jax.sharding import PartitionSpec as P

LANES = 128
IL_DEV = 2
XL_DEV = 8
CAP = 4
HALVES = 2
STEPS = 2
STRIDE = 33
MERGE = 4
F32 = jnp.float32
BF16 = jnp.bfloat16


def iota(shape, dim):
    return lax.broadcasted_iota(jnp.int32, shape, dim)


def woven(first, second):
    rows, width = first.shape
    first, second = first.reshape(rows // 8, 8, width), second.reshape(rows // 8, 8, width)
    low = iota(first.shape, 1) < CAP
    even = jnp.where(low, first, pltpu.roll(second, CAP, 1))
    odd = jnp.where(low, pltpu.roll(first, CAP, 1), second)
    return jnp.stack([even, odd], axis=1).reshape(2 * rows, width)


def apart(rows):
    count, width = rows.shape
    pairs = rows.astype(F32).reshape(count // 16, 2, 8, width)
    even, odd = pairs[:, 0], pairs[:, 1]
    low = iota(even.shape, 1) < CAP
    first = jnp.where(low, even, pltpu.roll(odd, CAP, 1))
    second = jnp.where(low, pltpu.roll(even, CAP, 1), odd)
    return first.reshape(count // 2, width), second.reshape(count // 2, width)


def send_kernel(traces, shot_filter, gain, owner, slot, offset, out, filtered):
    rows, samples = traces.shape
    blocks = samples // LANES
    half = samples // HALVES
    slots = slot[...]
    hi = (slots % XL_DEV) * IL_DEV + slots // XL_DEV
    lo = offset[...]
    lane_row = iota((LANES, rows), 0)
    table = jnp.where(lane_row == 0, 1.0, 0.0)
    table = jnp.where(lane_row == 1, jnp.broadcast_to(hi.astype(F32), table.shape), table)
    table = jnp.where(lane_row == 2, jnp.broadcast_to(lo.astype(F32), table.shape), table)
    table = jnp.where(lane_row == 3, jnp.broadcast_to(gain[...], table.shape), table)
    table = jnp.where(lane_row == 4, jnp.broadcast_to(owner[...].astype(F32), table.shape), table)
    columns = table.T
    gain_column = columns[:, 3:4]
    owner_column = columns[:, 4:5].astype(jnp.int32)
    codes = jnp.where(iota(columns.shape, 1) < 3, columns, 0.0).astype(BF16)
    owner_row = owner[...]
    same = (owner_column == owner_row) & (iota((rows, rows), 0) < iota((rows, rows), 1))
    rank = jnp.sum(jnp.where(same, 1.0, 0.0), axis=0, keepdims=True).astype(jnp.int32)
    row_ids = iota((out.shape[0] // HALVES, rows), 0)
    placed = jnp.where(row_ids == owner_row * CAP + rank, 1.0, 0.0).astype(BF16)
    taps = jnp.broadcast_to(shot_filter[...].astype(F32), (LANES, LANES))
    circulant = pltpu.roll(taps, 0, 1, stride=1, stride_axis=0)
    later = iota((LANES, LANES), 0) > iota((LANES, LANES), 1)
    before = jnp.where(later, circulant, 0.0).astype(BF16)
    centre = jnp.where(later, 0.0, circulant).astype(BF16)
    matrix = jnp.concatenate([before, centre], axis=0)
    for j in range(blocks):
        if j == 0:
            value = jnp.dot(traces[:, :LANES], centre, preferred_element_type=F32)
        else:
            value = jnp.dot(
                traces[:, (j - 1) * LANES : (j + 1) * LANES], matrix, preferred_element_type=F32
            )
        h, at = divmod(j * LANES, half)
        filtered[h * rows : (h + 1) * rows, at : at + LANES] = (value * gain_column).astype(BF16)
    width = 2 * LANES
    for n in range(0, half, width):
        parts = [
            jnp.dot(
                placed,
                filtered[h * rows : (h + 1) * rows, n : n + width],
                preferred_element_type=F32,
            )
            for h in range(HALVES)
        ]
        out[:, n : n + width] = woven(*parts).astype(BF16)
    part = jnp.dot(placed, codes, preferred_element_type=F32)
    out[:, half:] = woven(part, part).astype(BF16)


def stack_kernel(arrived, dip, start, weights, centre, right, left, binned, dips, dipped):
    slots = arrived.shape[0]
    half = arrived.shape[1] - LANES
    offsets, samples = start.shape
    blocks = samples // LANES
    lines = IL_DEV * offsets
    cells = XL_DEV * lines
    taps_x = dip.shape[0]
    rim = XL_DEV // 2
    out_lines = 2 * XL_DEV
    codes = apart(arrived[:, half:])[0]
    rows = codes.T
    code = jnp.where(rows[0:1] > 0.5, rows[1:2] * offsets + rows[2:3], -1.0).astype(jnp.int32)
    hit = iota((cells, slots // HALVES), 0) == code
    member = jnp.where(hit, 1.0, 0.0).astype(BF16)
    fold = jnp.dot(member, codes.astype(BF16), preferred_element_type=F32)[:, 0:1]
    scale = 1.0 / jnp.maximum(fold, 1.0)
    zero = jnp.zeros((XL_DEV, lines, LANES), BF16)
    binned[0] = zero
    binned[blocks + 1] = zero
    width = 2 * LANES
    for n in range(0, half, width):
        parts = apart(arrived[:, n : n + width])
        for h in range(HALVES):
            value = (
                jnp.dot(member, parts[h].astype(BF16), preferred_element_type=F32) * scale
            ).astype(BF16)
            for b in range(width // LANES):
                binned[(h * half + n) // LANES + b + 1] = value[
                    :, b * LANES : (b + 1) * LANES
                ].reshape(XL_DEV, lines, LANES)
    bands = []
    for a in range(taps_x):
        spread = jnp.broadcast_to(dip[a : a + 1, :], (2 * LANES, 2 * LANES))
        band = pltpu.roll(spread, 0, 1, stride=1, stride_axis=0)
        bands.append(band[:, :LANES].astype(BF16))
    none = jnp.zeros((2 * LANES, LANES), BF16)
    for d in range(taps_x + 1):
        dips[d * width : (d + 1) * width, :LANES] = bands[d] if d < taps_x else none
        dips[d * width : (d + 1) * width, LANES:] = bands[d - 1] if d > 0 else none

    group = dipped.shape[0] // STEPS

    def filter_group(g, carry):
        first = g * group
        for pair in range(out_lines // 2):
            low = max(0, 2 * pair - 2 * rim)
            high = min(XL_DEV, 2 * pair + 2)
            d = low - 2 * pair + 2 * rim
            lhs = jnp.concatenate(
                [
                    binned[pl.ds(first + b, group), x].reshape(group * lines, LANES)
                    for x in range(low, high)
                    for b in range(2)
                ],
                axis=1,
            )
            value = jnp.dot(
                lhs, dips[d * width : (d + high - low) * width, :], preferred_element_type=F32
            )
            for m in range(group):
                for i in range(IL_DEV):
                    for s in range(2):
                        line = (2 * pair + s - rim) % out_lines
                        at = m * lines + i * offsets
                        dipped[first + m, pl.ds(i * out_lines + line, offsets, stride=STRIDE), :] = (
                            value[at : at + offsets, s * LANES : (s + 1) * LANES]
                        )
        return carry

    lax.fori_loop(0, STEPS, filter_group, 0)

    tile = 8
    span = 2 * out_lines
    sublane = iota((tile, LANES), 0)
    root = 1.0 / math.sqrt(offsets)
    nothing = jnp.zeros((2 * tile, LANES), BF16)

    def move_out(j, carry):
        at = pl.multiple_of(j * LANES, LANES)
        firsts = start[:, pl.ds(at, LANES)] + (LANES // 2 - at)
        total = jnp.zeros((span, LANES), F32)
        lhs, band = [], []
        for o in range(offsets):
            first = jnp.broadcast_to(firsts[o : o + 1, :], (tile, LANES))
            turned = jnp.take_along_axis(
                weights[o, :, pl.ds(at, LANES)].astype(F32), (sublane - first) & (tile - 1), axis=0
            )
            turned = jnp.concatenate([turned, turned], axis=0).astype(BF16)
            place = ((first - sublane + (tile - 1)) >> 3).astype(F32)
            place = jnp.concatenate([place, place - 1.0], axis=0).astype(BF16)
            band += [
                jnp.where(place == float(g), turned, nothing)
                for g in range(0, 2 * LANES // tile, 2)
            ]
            rows = pl.ds(o * STRIDE, span)
            lhs += [dipped[j, rows, :].astype(BF16), dipped[j + 1, rows, :].astype(BF16)]
            if o % MERGE == MERGE - 1:
                total = total + jnp.dot(
                    jnp.concatenate(lhs, axis=1),
                    jnp.concatenate(band, axis=0),
                    preferred_element_type=F32,
                )
                lhs, band = [], []
        total = total * root
        for i in range(IL_DEV):
            base = i * out_lines
            centre[i, :, pl.ds(at, LANES)] = total[base : base + XL_DEV, :]
            right[i, :, pl.ds(at, LANES)] = total[base + XL_DEV : base + XL_DEV + rim, :]
            left[i, :, pl.ds(at, LANES)] = total[base + XL_DEV + rim : base + out_lines, :]
        return carry

    lax.fori_loop(0, blocks, move_out, 0)


def whole(count):
    return [pl.BlockSpec(memory_space=pltpu.VMEM)] * count


def send_call(traces, shot_filter, channel_gain, bin_owner, bin_slot, offset_class, owners):
    rows, samples = traces.shape
    width = samples // HALVES + LANES
    per_owner = CAP * HALVES
    return pl.pallas_call(
        send_kernel,
        out_shape=jax.ShapeDtypeStruct((owners * per_owner, width), BF16),
        in_specs=whole(6),
        out_specs=pl.BlockSpec(memory_space=pltpu.VMEM),
        scratch_shapes=[
            pltpu.VMEM((HALVES * rows, samples // HALVES), BF16),
        ],
        compiler_params=pltpu.CompilerParams(vmem_limit_bytes=16 * 2**20),
    )(
        traces,
        shot_filter,
        channel_gain.reshape(1, rows),
        bin_owner.reshape(1, rows),
        bin_slot.reshape(1, rows),
        offset_class.reshape(1, rows),
    )


def stack_call(arrived, dip_filter, nmo_start, nmo_weights):
    offsets, samples = nmo_start.shape
    taps_x, taps_t = dip_filter.shape
    begin = 2 * LANES - LANES // 2 - taps_t // 2
    spread = jnp.pad(
        dip_filter[:, ::-1].astype(F32), ((0, 0), (begin, 2 * LANES - begin - taps_t))
    )
    blocks = samples // LANES
    lines = IL_DEV * offsets
    edge = jax.ShapeDtypeStruct((IL_DEV, XL_DEV // 2, samples), F32)
    return pl.pallas_call(
        stack_kernel,
        out_shape=(jax.ShapeDtypeStruct((IL_DEV, XL_DEV, samples), F32), edge, edge),
        in_specs=whole(4),
        out_specs=tuple(whole(3)),
        scratch_shapes=[
            pltpu.VMEM((blocks + 3, XL_DEV, lines, LANES), BF16),
            pltpu.VMEM(((taps_x + 1) * 2 * LANES, 2 * LANES), BF16),
            pltpu.VMEM((blocks + 2, offsets * STRIDE, LANES), F32),
        ],
        compiler_params=pltpu.CompilerParams(vmem_limit_bytes=30 * 2**20),
    )(arrived, spread, nmo_start, nmo_weights)


def per_device(
    traces,
    shot_filter,
    channel_gain,
    bin_owner,
    bin_slot,
    offset_class,
    dip_filter,
    nmo_start,
    nmo_weights,
):
    owners = lax.axis_size("shot") * lax.axis_size("bin")
    outgoing = send_call(
        traces, shot_filter, channel_gain, bin_owner, bin_slot, offset_class, owners
    )
    rows, width = outgoing.shape
    arrived = lax.all_to_all(
        outgoing.reshape(owners, rows // owners, width), ("shot", "bin"), 0, 0, tiled=True
    ).reshape(rows, width)
    centre, right, left = stack_call(arrived, dip_filter, nmo_start, nmo_weights)
    count = lax.axis_size("bin")
    ends = range(count - 1)
    from_left = lax.ppermute(right, "bin", [(i, i + 1) for i in ends])
    from_right = lax.ppermute(left, "bin", [(i + 1, i) for i in ends])
    return centre + jnp.concatenate([from_left, from_right], axis=1)


def solution(mesh):
    placed = (
        P(("shot", "bin"), None),
        P(("shot", "bin"), None),
        P(),
        P(("shot", "bin"), None),
        P(("shot", "bin")),
        P(("shot", "bin")),
        P(),
        P(),
        P(),
    )
    return jax.shard_map(
        per_device, mesh=mesh, in_specs=placed, out_specs=P("shot", "bin", None), check_vma=False
    )
```

```python
import math

import jax
import jax.numpy as jnp
from jax import lax
from jax.experimental import pallas as pl
from jax.experimental.pallas import tpu as pltpu
from jax.sharding import PartitionSpec as P

LANES = 128
IL_DEV = 2
XL_DEV = 8
CAP = 4
HALVES = 2
STEPS = 2
STRIDE = 33
TAIL = 32
DIP_REACH = 15
MERGE = 4
F32 = jnp.float32
BF16 = jnp.bfloat16


def iota(shape, dim):
    return lax.broadcasted_iota(jnp.int32, shape, dim)


def woven(first, second):
    rows, width = first.shape
    first, second = first.reshape(rows // 8, 8, width), second.reshape(rows // 8, 8, width)
    low = iota(first.shape, 1) < CAP
    even = jnp.where(low, first, pltpu.roll(second, CAP, 1))
    odd = jnp.where(low, pltpu.roll(first, CAP, 1), second)
    return jnp.stack([even, odd], axis=1).reshape(2 * rows, width)


def apart(rows):
    count, width = rows.shape
    pairs = rows.astype(F32).reshape(count // 16, 2, 8, width)
    even, odd = pairs[:, 0], pairs[:, 1]
    low = iota(even.shape, 1) < CAP
    first = jnp.where(low, even, pltpu.roll(odd, CAP, 1))
    second = jnp.where(low, pltpu.roll(even, CAP, 1), odd)
    return first.reshape(count // 2, width), second.reshape(count // 2, width)


def send_kernel(
    traces_hbm, shot_filter, gain, owner, slot, offset, out_hbm, traces, out, filtered, sems
):
    rows, samples = traces.shape
    blocks = samples // LANES
    half = samples // HALVES
    fetch = pltpu.make_async_copy(traces_hbm, traces, sems.at[0])
    fetch.start()
    copies = []

    def send(n, stop):
        columns = (slice(None), slice(n, stop))
        copy = pltpu.make_async_copy(
            out.at[columns], out_hbm.at[columns], sems.at[1 + len(copies)]
        )
        copy.start()
        copies.append(copy)

    slots = slot[...]
    hi = (slots % XL_DEV) * IL_DEV + slots // XL_DEV
    lo = offset[...]
    lane_row = iota((LANES, rows), 0)
    table = jnp.where(lane_row == 0, 1.0, 0.0)
    table = jnp.where(lane_row == 1, jnp.broadcast_to(hi.astype(F32), table.shape), table)
    table = jnp.where(lane_row == 2, jnp.broadcast_to(lo.astype(F32), table.shape), table)
    table = jnp.where(lane_row == 3, jnp.broadcast_to(gain[...], table.shape), table)
    table = jnp.where(lane_row == 4, jnp.broadcast_to(owner[...].astype(F32), table.shape), table)
    columns = table.T
    gain_column = columns[:, 3:4]
    owner_column = columns[:, 4:5].astype(jnp.int32)
    codes = jnp.where(iota(columns.shape, 1) < 3, columns, 0.0).astype(BF16)
    owner_row = owner[...]
    same = (owner_column == owner_row) & (iota((rows, rows), 0) < iota((rows, rows), 1))
    rank = jnp.sum(jnp.where(same, 1.0, 0.0), axis=0, keepdims=True).astype(jnp.int32)
    row_ids = iota((out.shape[0] // HALVES, rows), 0)
    placed = jnp.where(row_ids == owner_row * CAP + rank, 1.0, 0.0).astype(BF16)
    taps = jnp.broadcast_to(shot_filter[...].astype(F32), (LANES, LANES))
    circulant = pltpu.roll(taps, 0, 1, stride=1, stride_axis=0)
    later = iota((LANES, LANES), 0) > iota((LANES, LANES), 1)
    before = jnp.where(later, circulant, 0.0).astype(BF16)
    centre = jnp.where(later, 0.0, circulant).astype(BF16)
    matrix = jnp.concatenate([before, centre], axis=0)
    part = jnp.dot(placed, codes, preferred_element_type=F32)
    out[:, half:] = woven(part, part).astype(BF16)
    send(half, half + LANES)
    fetch.wait()
    for j in range(blocks):
        if j == 0:
            value = jnp.dot(traces[:, :LANES], centre, preferred_element_type=F32)
        else:
            value = jnp.dot(
                traces[:, (j - 1) * LANES : (j + 1) * LANES], matrix, preferred_element_type=F32
            )
        h, at = divmod(j * LANES, half)
        filtered[h * rows : (h + 1) * rows, at : at + LANES] = (value * gain_column).astype(BF16)
    width = 2 * LANES
    for n in range(0, half, width):
        parts = [
            jnp.dot(
                placed,
                filtered[h * rows : (h + 1) * rows, n : n + width],
                preferred_element_type=F32,
            )
            for h in range(HALVES)
        ]
        out[:, n : n + width] = woven(*parts).astype(BF16)
        send(n, n + width)
    for copy in copies:
        copy.wait()


def prepare_kernel(dip, start, weights, heads, tails, turned, place):
    taps_x = dip.shape[0]
    offsets, samples = start.shape
    bands = []
    for a in range(taps_x):
        spread = jnp.broadcast_to(dip[a : a + 1, :], (LANES + TAIL, 2 * LANES))
        bands.append(pltpu.roll(spread, 1, 1, stride=1, stride_axis=0)[:, :LANES].astype(BF16))
    none = jnp.zeros((LANES + TAIL, LANES), BF16)
    for d in range(-2, taps_x + 3):
        pair = [bands[a] if 0 <= a < taps_x else none for a in (d, d - 1)]
        for s in range(2):
            lanes = slice(s * LANES, (s + 1) * LANES)
            if 0 <= d <= taps_x:
                heads[d * LANES : (d + 1) * LANES, lanes] = pair[s][:LANES]
            tails[(d + 2) * TAIL : (d + 3) * TAIL, lanes] = pair[s][LANES:]
    tile = 8
    sublane = iota((tile, LANES), 0)

    def offset_bands(j, carry):
        at = pl.multiple_of(j * LANES, LANES)
        firsts = start[:, pl.ds(at, LANES)] + (LANES - DIP_REACH - at)
        for o in range(offsets):
            first = jnp.broadcast_to(firsts[o : o + 1, :], (tile, LANES))
            weight = jnp.take_along_axis(
                weights[o, :, pl.ds(at, LANES)].astype(F32), (sublane - first) & (tile - 1), axis=0
            )
            group = ((first - sublane + (tile - 1)) >> 3).astype(F32)
            rows = slice(o * tile, (o + 1) * tile)
            turned[j, rows, :] = weight
            place[j, rows, :] = group
        return carry

    lax.fori_loop(0, samples // LANES, offset_bands, 0)


def stack_kernel(
    arrived, heads, tails, turned, place, centre, right, left, binned, ends, dipped
):
    slots = arrived.shape[0]
    half = arrived.shape[1] - LANES
    blocks = turned.shape[0]
    offsets = turned.shape[1] // 8
    lines = IL_DEV * offsets
    cells = XL_DEV * lines
    rim = XL_DEV // 2
    out_lines = 2 * XL_DEV
    codes = apart(arrived[:, half:])[0]
    rows = codes.T
    code = jnp.where(rows[0:1] > 0.5, rows[1:2] * offsets + rows[2:3], -1.0).astype(jnp.int32)
    hit = iota((cells, slots // HALVES), 0) == code
    member = jnp.where(hit, 1.0, 0.0).astype(BF16)
    fold = jnp.dot(member, codes.astype(BF16), preferred_element_type=F32)[:, 0:1]
    scale = 1.0 / jnp.maximum(fold, 1.0)
    binned[0] = jnp.zeros((XL_DEV, lines, LANES), BF16)
    binned[blocks + 1] = jnp.zeros((XL_DEV, lines, LANES), BF16)
    ends[blocks + 1] = jnp.zeros((2, lines, LANES), BF16)
    width = 2 * LANES
    lane = iota((lines, LANES), 1)
    for n in range(0, half, width):
        parts = apart(arrived[:, n : n + width])
        for h in range(HALVES):
            value = (
                jnp.dot(member, parts[h].astype(BF16), preferred_element_type=F32) * scale
            )
            for b in range(width // LANES):
                at = (h * half + n) // LANES + b + 1
                block = value[:, b * LANES : (b + 1) * LANES]
                binned[at] = block.astype(BF16).reshape(XL_DEV, lines, LANES)
                for g in range(2):
                    end = block[g * rim * lines : (g * rim + 1) * lines]
                    for x in range(1, rim):
                        line = block[(g * rim + x) * lines : (g * rim + x + 1) * lines]
                        end = jnp.where(lane < x * TAIL, end, pltpu.roll(line, x * TAIL, 1))
                    ends[at, g] = end.astype(BF16)

    group = dipped.shape[0] // STEPS

    def filter_group(step, carry):
        first = step * group
        for pair in range(out_lines // 2):
            low = max(0, 2 * pair - 2 * rim)
            high = min(XL_DEV, 2 * pair + 2)
            d = low - 2 * pair + 2 * rim
            lhs = [
                binned[pl.ds(first, group), x].reshape(group * lines, LANES)
                for x in range(low, high)
            ]
            rhs = [heads[d * LANES : (d + high - low) * LANES, :]]
            for g in range(2):
                if low < (g + 1) * rim and high > g * rim:
                    d = g * rim - 2 * pair + 2 * rim + 2
                    lhs.append(ends[pl.ds(first + 1, group), g].reshape(group * lines, LANES))
                    rhs.append(tails[d * TAIL : (d + rim) * TAIL, :])
            value = jnp.dot(
                jnp.concatenate(lhs, axis=1),
                jnp.concatenate(rhs, axis=0),
                preferred_element_type=F32,
            )
            for m in range(group):
                for i in range(IL_DEV):
                    for s in range(2):
                        line = (2 * pair + s - rim) % out_lines
                        at = m * lines + i * offsets
                        to = pl.ds(i * out_lines + line, offsets, stride=STRIDE)
                        dipped[first + m, to, :] = value[
                            at : at + offsets, s * LANES : (s + 1) * LANES
                        ]
        return carry

    lax.fori_loop(0, STEPS, filter_group, 0)

    span = 2 * out_lines
    root = 1.0 / math.sqrt(offsets)
    tile = 8
    nothing = jnp.zeros((2 * tile, LANES), BF16)

    def move_out(j, carry):
        at = pl.multiple_of(j * LANES, LANES)
        total = jnp.zeros((span, LANES), F32)
        lhs, band = [], []
        for o in range(offsets):
            weight = turned[j, o * tile : (o + 1) * tile, :]
            weight = jnp.concatenate([weight, weight], axis=0).astype(BF16)
            group = place[j, o * tile : (o + 1) * tile, :]
            group = jnp.concatenate([group, group - 1.0], axis=0).astype(BF16)
            band += [jnp.where(group == float(g), weight, nothing) for g in range(0, 32, 2)]
            rows = pl.ds(o * STRIDE, span)
            lhs += [dipped[j, rows, :].astype(BF16), dipped[j + 1, rows, :].astype(BF16)]
            if o % MERGE == MERGE - 1:
                total = total + jnp.dot(
                    jnp.concatenate(lhs, axis=1),
                    jnp.concatenate(band, axis=0),
                    preferred_element_type=F32,
                )
                lhs, band = [], []
        total = total * root
        for i in range(IL_DEV):
            base = i * out_lines
            edge = pl.ds(i * rim, rim)
            centre[i, :, pl.ds(at, LANES)] = total[base : base + XL_DEV, :]
            right[edge, pl.ds(at, LANES)] = total[base + XL_DEV : base + XL_DEV + rim, :]
            left[edge, pl.ds(at, LANES)] = total[base + XL_DEV + rim : base + out_lines, :]
        return carry

    lax.fori_loop(0, blocks, move_out, 0)


def whole(count):
    return [pl.BlockSpec(memory_space=pltpu.VMEM)] * count


def send_call(traces, shot_filter, channel_gain, bin_owner, bin_slot, offset_class, owners):
    rows, samples = traces.shape
    width = samples // HALVES + LANES
    per_owner = CAP * HALVES
    return pl.pallas_call(
        send_kernel,
        out_shape=jax.ShapeDtypeStruct((owners * per_owner, width), BF16),
        in_specs=[pl.BlockSpec(memory_space=pl.ANY)] + whole(5),
        out_specs=pl.BlockSpec(memory_space=pl.ANY),
        scratch_shapes=[
            pltpu.VMEM((rows, samples), BF16),
            pltpu.VMEM((owners * per_owner, width), BF16),
            pltpu.VMEM((HALVES * rows, samples // HALVES), BF16),
            pltpu.SemaphoreType.DMA((2 + samples // HALVES // (2 * LANES),)),
        ],
    )(
        traces,
        shot_filter,
        channel_gain.reshape(1, rows),
        bin_owner.reshape(1, rows),
        bin_slot.reshape(1, rows),
        offset_class.reshape(1, rows),
    )


def prepare_call(dip_filter, nmo_start, nmo_weights):
    offsets, samples = nmo_start.shape
    taps_x, taps_t = dip_filter.shape
    spread = jnp.pad(dip_filter[:, ::-1].astype(F32), ((0, 0), (2 * LANES - taps_t, 0)))
    band = jax.ShapeDtypeStruct((samples // LANES, offsets * 8, LANES), F32)
    return pl.pallas_call(
        prepare_kernel,
        out_shape=(
            jax.ShapeDtypeStruct(((taps_x + 1) * LANES, 2 * LANES), BF16),
            jax.ShapeDtypeStruct(((taps_x + 5) * TAIL, 2 * LANES), BF16),
            band,
            band,
        ),
        in_specs=whole(3),
        out_specs=tuple(whole(4)),
        compiler_params=pltpu.CompilerParams(vmem_limit_bytes=20 * 2**20),
    )(spread, nmo_start, nmo_weights)


def stack_call(arrived, heads, tails, turned, place):
    blocks = turned.shape[0]
    offsets = turned.shape[1] // 8
    samples = blocks * LANES
    lines = IL_DEV * offsets
    edge = jax.ShapeDtypeStruct((IL_DEV * XL_DEV // 2, samples), F32)
    return pl.pallas_call(
        stack_kernel,
        out_shape=(jax.ShapeDtypeStruct((IL_DEV, XL_DEV, samples), F32), edge, edge),
        in_specs=whole(5),
        out_specs=tuple(whole(3)),
        scratch_shapes=[
            pltpu.VMEM((blocks + 2, XL_DEV, lines, LANES), BF16),
            pltpu.VMEM((blocks + 3, 2, lines, LANES), BF16),
            pltpu.VMEM((blocks + 2, offsets * STRIDE, LANES), F32),
        ],
        compiler_params=pltpu.CompilerParams(vmem_limit_bytes=30 * 2**20),
    )(arrived, heads, tails, turned, place)


def per_device(
    traces,
    shot_filter,
    channel_gain,
    bin_owner,
    bin_slot,
    offset_class,
    dip_filter,
    nmo_start,
    nmo_weights,
):
    owners = lax.axis_size("shot") * lax.axis_size("bin")
    outgoing = send_call(
        traces, shot_filter, channel_gain, bin_owner, bin_slot, offset_class, owners
    )
    rows, width = outgoing.shape
    arrived = lax.all_to_all(
        outgoing.reshape(owners, rows // owners, width), ("shot", "bin"), 0, 0, tiled=True
    ).reshape(rows, width)
    prepared = prepare_call(dip_filter, nmo_start, nmo_weights)
    centre, right, left = stack_call(arrived, *prepared)
    count = lax.axis_size("bin")
    ends = range(count - 1)
    from_left = lax.ppermute(right, "bin", [(i, i + 1) for i in ends])
    from_right = lax.ppermute(left, "bin", [(i + 1, i) for i in ends])
    shape = (IL_DEV, XL_DEV // 2, centre.shape[2])
    return centre + jnp.concatenate(
        [from_left.reshape(shape), from_right.reshape(shape)], axis=1
    )


def solution(mesh):
    placed = (
        P(("shot", "bin"), None),
        P(("shot", "bin"), None),
        P(),
        P(("shot", "bin"), None),
        P(("shot", "bin")),
        P(("shot", "bin")),
        P(),
        P(),
        P(),
    )
    return jax.shard_map(
        per_device, mesh=mesh, in_specs=placed, out_specs=P("shot", "bin", None), check_vma=False
    )
```

```python
import math

import jax
import jax.numpy as jnp
from jax import lax
from jax.experimental import pallas as pl
from jax.experimental.pallas import tpu as pltpu
from jax.sharding import PartitionSpec as P

LANES = 128
IL_DEV = 2
XL_DEV = 8
CAP = 4
HALVES = 2
STEPS = 2
STRIDE = 33
TAIL = 32
DIP_REACH = 15
FILTER_ROWS = 4096
MERGE = 4
F32 = jnp.float32
BF16 = jnp.bfloat16


def iota(shape, dim):
    return lax.broadcasted_iota(jnp.int32, shape, dim)


def woven(first, second):
    rows, width = first.shape
    first, second = first.reshape(rows // 8, 8, width), second.reshape(rows // 8, 8, width)
    low = iota(first.shape, 1) < CAP
    even = jnp.where(low, first, pltpu.roll(second, CAP, 1))
    odd = jnp.where(low, pltpu.roll(first, CAP, 1), second)
    return jnp.stack([even, odd], axis=1).reshape(2 * rows, width)


def apart(rows):
    count, width = rows.shape
    pairs = rows.astype(F32).reshape(count // 16, 2, 8, width)
    even, odd = pairs[:, 0], pairs[:, 1]
    low = iota(even.shape, 1) < CAP
    first = jnp.where(low, even, pltpu.roll(odd, CAP, 1))
    second = jnp.where(low, pltpu.roll(even, CAP, 1), odd)
    return first.reshape(count // 2, width), second.reshape(count // 2, width)


def send_kernel(
    traces_hbm, shot_filter, gain, owner, slot, offset, out_hbm, traces, out, filtered, sems
):
    rows, samples = traces.shape
    blocks = samples // LANES
    half = samples // HALVES
    fetch = pltpu.make_async_copy(traces_hbm, traces, sems.at[0])
    fetch.start()
    copies = []

    def send(n, stop):
        columns = (slice(None), slice(n, stop))
        copy = pltpu.make_async_copy(
            out.at[columns], out_hbm.at[columns], sems.at[1 + len(copies)]
        )
        copy.start()
        copies.append(copy)

    slots = slot[...]
    hi = (slots % XL_DEV) * IL_DEV + slots // XL_DEV
    lo = offset[...]
    lane_row = iota((LANES, rows), 0)
    table = jnp.where(lane_row == 0, 1.0, 0.0)
    table = jnp.where(lane_row == 1, jnp.broadcast_to(hi.astype(F32), table.shape), table)
    table = jnp.where(lane_row == 2, jnp.broadcast_to(lo.astype(F32), table.shape), table)
    table = jnp.where(lane_row == 3, jnp.broadcast_to(gain[...], table.shape), table)
    table = jnp.where(lane_row == 4, jnp.broadcast_to(owner[...].astype(F32), table.shape), table)
    columns = table.T
    gain_column = columns[:, 3:4]
    owner_column = columns[:, 4:5].astype(jnp.int32)
    codes = jnp.where(iota(columns.shape, 1) < 3, columns, 0.0).astype(BF16)
    owner_row = owner[...]
    same = (owner_column == owner_row) & (iota((rows, rows), 0) < iota((rows, rows), 1))
    rank = jnp.sum(jnp.where(same, 1.0, 0.0), axis=0, keepdims=True).astype(jnp.int32)
    row_ids = iota((out.shape[0] // HALVES, rows), 0)
    placed = jnp.where(row_ids == owner_row * CAP + rank, 1.0, 0.0).astype(BF16)
    taps = jnp.broadcast_to(shot_filter[...].astype(F32), (LANES, LANES))
    circulant = pltpu.roll(taps, 0, 1, stride=1, stride_axis=0)
    later = iota((LANES, LANES), 0) > iota((LANES, LANES), 1)
    before = jnp.where(later, circulant, 0.0).astype(BF16)
    centre = jnp.where(later, 0.0, circulant).astype(BF16)
    matrix = jnp.concatenate([before, centre], axis=0)
    part = jnp.dot(placed, codes, preferred_element_type=F32)
    out[:, half:] = woven(part, part).astype(BF16)
    send(half, half + LANES)
    fetch.wait()
    for j in range(blocks):
        if j == 0:
            value = jnp.dot(traces[:, :LANES], centre, preferred_element_type=F32)
        else:
            value = jnp.dot(
                traces[:, (j - 1) * LANES : (j + 1) * LANES], matrix, preferred_element_type=F32
            )
        h, at = divmod(j * LANES, half)
        filtered[h * rows : (h + 1) * rows, at : at + LANES] = (value * gain_column).astype(BF16)
    width = 2 * LANES
    for n in range(0, half, width):
        parts = [
            jnp.dot(
                placed,
                filtered[h * rows : (h + 1) * rows, n : n + width],
                preferred_element_type=F32,
            )
            for h in range(HALVES)
        ]
        out[:, n : n + width] = woven(*parts).astype(BF16)
        send(n, n + width)
    for copy in copies:
        copy.wait()


def prepare_kernel(dip, start, weights, filters, moves):
    taps_x = dip.shape[0]
    offsets, samples = start.shape
    bands = []
    for a in range(taps_x):
        spread = jnp.broadcast_to(dip[a : a + 1, :], (LANES + TAIL, 2 * LANES))
        bands.append(pltpu.roll(spread, 1, 1, stride=1, stride_axis=0)[:, :LANES].astype(BF16))
    none = jnp.zeros((LANES + TAIL, LANES), BF16)
    for d in range(-2, taps_x + 3):
        pair = [bands[a] if 0 <= a < taps_x else none for a in (d, d - 1)]
        for s in range(2):
            lanes = slice(s * LANES, (s + 1) * LANES)
            if 0 <= d <= taps_x:
                filters[d * LANES : (d + 1) * LANES, lanes] = pair[s][:LANES]
            tail = (taps_x + 1) * LANES + (d + 2) * TAIL
            filters[tail : tail + TAIL, lanes] = pair[s][LANES:]
    tile = 8
    sublane = iota((tile, LANES), 0)

    def offset_bands(j, carry):
        at = pl.multiple_of(j * LANES, LANES)
        firsts = start[:, pl.ds(at, LANES)] + (LANES - DIP_REACH - at)
        for o in range(offsets):
            first = jnp.broadcast_to(firsts[o : o + 1, :], (tile, LANES))
            weight = jnp.take_along_axis(
                weights[o, :, pl.ds(at, LANES)].astype(F32), (sublane - first) & (tile - 1), axis=0
            )
            group = ((first - sublane + (tile - 1)) >> 3).astype(F32)
            row = 2 * o * tile
            moves[j, row : row + tile, :] = weight
            moves[j, row + tile : row + 2 * tile, :] = group
        return carry

    lax.fori_loop(0, samples // LANES, offset_bands, 0)


def stack_kernel(
    arrived_hbm,
    filters_hbm,
    moves_hbm,
    centre,
    right,
    left,
    arrived,
    filters,
    moves,
    binned,
    ends,
    dipped,
    sems,
):
    slots = arrived.shape[0]
    half = arrived.shape[1] - LANES
    width = 2 * LANES
    parts = [(half, half + LANES)] + [(n, n + width) for n in range(0, half, width)]
    pieces = [
        (arrived_hbm.at[:, start:stop], arrived.at[:, start:stop]) for start, stop in parts
    ]
    pieces += [(filters_hbm.at[: filters.shape[0]], filters), (moves_hbm, moves)]
    copies = [
        pltpu.make_async_copy(source, target, sems.at[i])
        for i, (source, target) in enumerate(pieces)
    ]
    for copy in copies:
        copy.start()
    blocks = moves.shape[0]
    offsets = moves.shape[1] // 16
    lines = IL_DEV * offsets
    cells = XL_DEV * lines
    rim = XL_DEV // 2
    out_lines = 2 * XL_DEV
    copies.pop(0).wait()
    codes = apart(arrived[:, half:])[0]
    rows = codes.T
    code = jnp.where(rows[0:1] > 0.5, rows[1:2] * offsets + rows[2:3], -1.0).astype(jnp.int32)
    hit = iota((cells, slots // HALVES), 0) == code
    member = jnp.where(hit, 1.0, 0.0).astype(BF16)
    fold = jnp.dot(member, codes.astype(BF16), preferred_element_type=F32)[:, 0:1]
    scale = 1.0 / jnp.maximum(fold, 1.0)
    binned[0] = jnp.zeros((XL_DEV, lines, LANES), BF16)
    binned[blocks + 1] = jnp.zeros((XL_DEV, lines, LANES), BF16)
    ends[blocks + 1] = jnp.zeros((2, lines, LANES), BF16)
    lane = iota((lines, LANES), 1)
    for n in range(0, half, width):
        copies.pop(0).wait()
        parts = apart(arrived[:, n : n + width])
        for h in range(HALVES):
            value = (
                jnp.dot(member, parts[h].astype(BF16), preferred_element_type=F32) * scale
            )
            for b in range(width // LANES):
                at = (h * half + n) // LANES + b + 1
                block = value[:, b * LANES : (b + 1) * LANES]
                binned[at] = block.astype(BF16).reshape(XL_DEV, lines, LANES)
                for g in range(2):
                    end = block[g * rim * lines : (g * rim + 1) * lines]
                    for x in range(1, rim):
                        line = block[(g * rim + x) * lines : (g * rim + x + 1) * lines]
                        end = jnp.where(lane < x * TAIL, end, pltpu.roll(line, x * TAIL, 1))
                    ends[at, g] = end.astype(BF16)

    copies.pop(0).wait()
    group = dipped.shape[0] // STEPS

    tails = (2 * rim + 2) * LANES

    def filter_group(step, carry):
        first = step * group
        for pair in range(out_lines // 2):
            low = max(0, 2 * pair - 2 * rim)
            high = min(XL_DEV, 2 * pair + 2)
            d = low - 2 * pair + 2 * rim
            lhs = [
                binned[pl.ds(first, group), x].reshape(group * lines, LANES)
                for x in range(low, high)
            ]
            rhs = [filters[d * LANES : (d + high - low) * LANES, :]]
            for g in range(2):
                if low < (g + 1) * rim and high > g * rim:
                    tail = tails + (g * rim - 2 * pair + 2 * rim + 2) * TAIL
                    lhs.append(ends[pl.ds(first + 1, group), g].reshape(group * lines, LANES))
                    rhs.append(filters[tail : tail + rim * TAIL, :])
            value = jnp.dot(
                jnp.concatenate(lhs, axis=1),
                jnp.concatenate(rhs, axis=0),
                preferred_element_type=F32,
            )
            for m in range(group):
                for i in range(IL_DEV):
                    for s in range(2):
                        line = (2 * pair + s - rim) % out_lines
                        at = m * lines + i * offsets
                        to = pl.ds(i * out_lines + line, offsets, stride=STRIDE)
                        dipped[first + m, to, :] = value[
                            at : at + offsets, s * LANES : (s + 1) * LANES
                        ]
        return carry

    lax.fori_loop(0, STEPS, filter_group, 0)
    copies.pop(0).wait()

    span = 2 * out_lines
    root = 1.0 / math.sqrt(offsets)
    tile = 8
    nothing = jnp.zeros((2 * tile, LANES), BF16)

    def move_out(j, carry):
        at = pl.multiple_of(j * LANES, LANES)
        total = jnp.zeros((span, LANES), F32)
        lhs, band = [], []
        for o in range(offsets):
            row = 2 * o * tile
            weight = moves[j, row : row + tile, :]
            weight = jnp.concatenate([weight, weight], axis=0).astype(BF16)
            group = moves[j, row + tile : row + 2 * tile, :]
            group = jnp.concatenate([group, group - 1.0], axis=0).astype(BF16)
            band += [jnp.where(group == float(g), weight, nothing) for g in range(0, 32, 2)]
            rows = pl.ds(o * STRIDE, span)
            lhs += [dipped[j, rows, :].astype(BF16), dipped[j + 1, rows, :].astype(BF16)]
            if o % MERGE == MERGE - 1:
                total = total + jnp.dot(
                    jnp.concatenate(lhs, axis=1),
                    jnp.concatenate(band, axis=0),
                    preferred_element_type=F32,
                )
                lhs, band = [], []
        total = total * root
        for i in range(IL_DEV):
            base = i * out_lines
            edge = pl.ds(i * rim, rim)
            centre[i, :, pl.ds(at, LANES)] = total[base : base + XL_DEV, :]
            right[edge, pl.ds(at, LANES)] = total[base + XL_DEV : base + XL_DEV + rim, :]
            left[edge, pl.ds(at, LANES)] = total[base + XL_DEV + rim : base + out_lines, :]
        return carry

    lax.fori_loop(0, blocks, move_out, 0)


def whole(count):
    return [pl.BlockSpec(memory_space=pltpu.VMEM)] * count


def send_call(traces, shot_filter, channel_gain, bin_owner, bin_slot, offset_class, owners):
    rows, samples = traces.shape
    width = samples // HALVES + LANES
    per_owner = CAP * HALVES
    return pl.pallas_call(
        send_kernel,
        out_shape=jax.ShapeDtypeStruct((owners * per_owner, width), BF16),
        in_specs=[pl.BlockSpec(memory_space=pl.ANY)] + whole(5),
        out_specs=pl.BlockSpec(memory_space=pl.ANY),
        scratch_shapes=[
            pltpu.VMEM((rows, samples), BF16),
            pltpu.VMEM((owners * per_owner, width), BF16),
            pltpu.VMEM((HALVES * rows, samples // HALVES), BF16),
            pltpu.SemaphoreType.DMA((2 + samples // HALVES // (2 * LANES),)),
        ],
    )(
        traces,
        shot_filter,
        channel_gain.reshape(1, rows),
        bin_owner.reshape(1, rows),
        bin_slot.reshape(1, rows),
        offset_class.reshape(1, rows),
    )


def prepare_call(dip_filter, nmo_start, nmo_weights):
    offsets, samples = nmo_start.shape
    taps_x, taps_t = dip_filter.shape
    spread = jnp.pad(dip_filter[:, ::-1].astype(F32), ((0, 0), (2 * LANES - taps_t, 0)))
    return pl.pallas_call(
        prepare_kernel,
        out_shape=(
            jax.ShapeDtypeStruct((FILTER_ROWS, 2 * LANES), BF16),
            jax.ShapeDtypeStruct((samples // LANES, offsets * 16, LANES), F32),
        ),
        in_specs=whole(3),
        out_specs=tuple(whole(2)),
        compiler_params=pltpu.CompilerParams(vmem_limit_bytes=20 * 2**20),
    )(spread, nmo_start, nmo_weights)


def stack_call(arrived, filters, moves):
    blocks = moves.shape[0]
    offsets = moves.shape[1] // 16
    samples = blocks * LANES
    lines = IL_DEV * offsets
    edge = jax.ShapeDtypeStruct((IL_DEV * XL_DEV // 2, samples), F32)
    return pl.pallas_call(
        stack_kernel,
        out_shape=(jax.ShapeDtypeStruct((IL_DEV, XL_DEV, samples), F32), edge, edge),
        in_specs=[pl.BlockSpec(memory_space=pl.ANY)] * 3,
        out_specs=tuple(whole(3)),
        scratch_shapes=[
            pltpu.VMEM(arrived.shape, BF16),
            pltpu.VMEM(((XL_DEV + 2) * LANES + (XL_DEV + 6) * TAIL, 2 * LANES), BF16),
            pltpu.VMEM(moves.shape, F32),
            pltpu.VMEM((blocks + 2, XL_DEV, lines, LANES), BF16),
            pltpu.VMEM((blocks + 3, 2, lines, LANES), BF16),
            pltpu.VMEM((blocks + 2, offsets * STRIDE, LANES), F32),
            pltpu.SemaphoreType.DMA((3 + samples // HALVES // (2 * LANES),)),
        ],
        compiler_params=pltpu.CompilerParams(vmem_limit_bytes=50 * 2**20),
    )(arrived, filters, moves)


def per_device(
    traces,
    shot_filter,
    channel_gain,
    bin_owner,
    bin_slot,
    offset_class,
    dip_filter,
    nmo_start,
    nmo_weights,
):
    owners = lax.axis_size("shot") * lax.axis_size("bin")
    outgoing = send_call(
        traces, shot_filter, channel_gain, bin_owner, bin_slot, offset_class, owners
    )
    rows, width = outgoing.shape
    arrived = lax.all_to_all(
        outgoing.reshape(owners, rows // owners, width), ("shot", "bin"), 0, 0, tiled=True
    ).reshape(rows, width)
    prepared = prepare_call(dip_filter, nmo_start, nmo_weights)
    centre, right, left = stack_call(arrived, *prepared)
    count = lax.axis_size("bin")
    ends = range(count - 1)
    from_left = lax.ppermute(right, "bin", [(i, i + 1) for i in ends])
    from_right = lax.ppermute(left, "bin", [(i + 1, i) for i in ends])
    shape = (IL_DEV, XL_DEV // 2, centre.shape[2])
    return centre + jnp.concatenate(
        [from_left.reshape(shape), from_right.reshape(shape)], axis=1
    )


def solution(mesh):
    placed = (
        P(("shot", "bin"), None),
        P(("shot", "bin"), None),
        P(),
        P(("shot", "bin"), None),
        P(("shot", "bin")),
        P(("shot", "bin")),
        P(),
        P(),
        P(),
    )
    return jax.shard_map(
        per_device, mesh=mesh, in_specs=placed, out_specs=P("shot", "bin", None), check_vma=False
    )
```

```python
import math

import jax
import jax.numpy as jnp
from jax import lax
from jax.experimental import pallas as pl
from jax.experimental.pallas import tpu as pltpu
from jax.sharding import PartitionSpec as P

LANES = 128
IL_DEV = 2
XL_DEV = 8
CAP = 4
HALVES = 2
STEPS = 2
STRIDE = 33
TAIL = 32
DIP_REACH = 15
FILTER_ROWS = 8192
MERGE = 4
F32 = jnp.float32
BF16 = jnp.bfloat16


def iota(shape, dim):
    return lax.broadcasted_iota(jnp.int32, shape, dim)


def woven(first, second):
    rows, width = first.shape
    first, second = first.reshape(rows // 8, 8, width), second.reshape(rows // 8, 8, width)
    low = iota(first.shape, 1) < CAP
    even = jnp.where(low, first, pltpu.roll(second, CAP, 1))
    odd = jnp.where(low, pltpu.roll(first, CAP, 1), second)
    return jnp.stack([even, odd], axis=1).reshape(2 * rows, width)


def apart(rows):
    count, width = rows.shape
    pairs = rows.astype(F32).reshape(count // 16, 2, 8, width)
    even, odd = pairs[:, 0], pairs[:, 1]
    low = iota(even.shape, 1) < CAP
    first = jnp.where(low, even, pltpu.roll(odd, CAP, 1))
    second = jnp.where(low, pltpu.roll(even, CAP, 1), odd)
    return first.reshape(count // 2, width), second.reshape(count // 2, width)


def send_kernel(
    traces_hbm,
    shot_filter_hbm,
    gain_hbm,
    owner_hbm,
    slot_hbm,
    offset_hbm,
    out_hbm,
    shot_filter,
    gain,
    owner,
    slot,
    offset,
    traces,
    out,
    filtered,
    sems,
    small_sems,
):
    rows, samples = traces.shape
    blocks = samples // LANES
    half = samples // HALVES
    pieces = [
        (owner_hbm, owner),
        (slot_hbm, slot),
        (offset_hbm, offset),
        (gain_hbm, gain),
        (shot_filter_hbm, shot_filter),
    ]
    small = [
        pltpu.make_async_copy(source, target, small_sems.at[i])
        for i, (source, target) in enumerate(pieces)
    ]
    for copy in small:
        copy.start()
    fetch = pltpu.make_async_copy(traces_hbm, traces, sems.at[0])
    fetch.start()
    copies = []

    def send(n, stop):
        columns = (slice(None), slice(n, stop))
        copy = pltpu.make_async_copy(
            out.at[columns], out_hbm.at[columns], sems.at[1 + len(copies)]
        )
        copy.start()
        copies.append(copy)

    for copy in small:
        copy.wait()
    slots = slot[...]
    hi = (slots % XL_DEV) * IL_DEV + slots // XL_DEV
    lo = offset[...]
    lane_row = iota((LANES, rows), 0)
    table = jnp.where(lane_row == 0, 1.0, 0.0)
    table = jnp.where(lane_row == 1, jnp.broadcast_to(hi.astype(F32), table.shape), table)
    table = jnp.where(lane_row == 2, jnp.broadcast_to(lo.astype(F32), table.shape), table)
    table = jnp.where(lane_row == 3, jnp.broadcast_to(gain[...], table.shape), table)
    table = jnp.where(lane_row == 4, jnp.broadcast_to(owner[...].astype(F32), table.shape), table)
    columns = table.T
    gain_column = columns[:, 3:4]
    owner_column = columns[:, 4:5].astype(jnp.int32)
    codes = jnp.where(iota(columns.shape, 1) < 3, columns, 0.0).astype(BF16)
    owner_row = owner[...]
    same = (owner_column == owner_row) & (iota((rows, rows), 0) < iota((rows, rows), 1))
    rank = jnp.sum(jnp.where(same, 1.0, 0.0), axis=0, keepdims=True).astype(jnp.int32)
    row_ids = iota((out.shape[0] // HALVES, rows), 0)
    placed = jnp.where(row_ids == owner_row * CAP + rank, 1.0, 0.0).astype(BF16)
    taps = jnp.broadcast_to(shot_filter[...].astype(F32), (LANES, LANES))
    circulant = pltpu.roll(taps, 0, 1, stride=1, stride_axis=0)
    later = iota((LANES, LANES), 0) > iota((LANES, LANES), 1)
    before = jnp.where(later, circulant, 0.0).astype(BF16)
    centre = jnp.where(later, 0.0, circulant).astype(BF16)
    matrix = jnp.concatenate([before, centre], axis=0)
    part = jnp.dot(placed, codes, preferred_element_type=F32)
    out[:, half:] = woven(part, part).astype(BF16)
    send(half, half + LANES)
    fetch.wait()
    for j in range(blocks):
        if j == 0:
            value = jnp.dot(traces[:, :LANES], centre, preferred_element_type=F32)
        else:
            value = jnp.dot(
                traces[:, (j - 1) * LANES : (j + 1) * LANES], matrix, preferred_element_type=F32
            )
        h, at = divmod(j * LANES, half)
        filtered[h * rows : (h + 1) * rows, at : at + LANES] = (value * gain_column).astype(BF16)
    width = 2 * LANES
    for n in range(0, half, width):
        parts = [
            jnp.dot(
                placed,
                filtered[h * rows : (h + 1) * rows, n : n + width],
                preferred_element_type=F32,
            )
            for h in range(HALVES)
        ]
        out[:, n : n + width] = woven(*parts).astype(BF16)
        send(n, n + width)
    for copy in copies:
        copy.wait()


def prepare_kernel(dip, start, weights, filters, moves):
    taps_x = dip.shape[0]
    offsets, samples = start.shape
    bands = []
    for a in range(taps_x):
        spread = jnp.broadcast_to(dip[a : a + 1, :], (LANES + TAIL, 2 * LANES))
        bands.append(pltpu.roll(spread, 1, 1, stride=1, stride_axis=0)[:, :LANES].astype(BF16))
    none = jnp.zeros((LANES + TAIL, LANES), BF16)
    for d in range(-2, taps_x + 3):
        pair = [bands[a] if 0 <= a < taps_x else none for a in (d, d - 1)]
        for s in range(2):
            lanes = slice(s * LANES, (s + 1) * LANES)
            if 0 <= d <= taps_x:
                filters[d * LANES : (d + 1) * LANES, lanes] = pair[s][:LANES]
            tail = (taps_x + 1) * LANES + (d + 2) * TAIL
            filters[tail : tail + TAIL, lanes] = pair[s][LANES:]
    tile = 8
    sublane = iota((tile, LANES), 0)

    def offset_bands(j, carry):
        at = pl.multiple_of(j * LANES, LANES)
        firsts = start[:, pl.ds(at, LANES)] + (LANES - DIP_REACH - at)
        for o in range(offsets):
            first = jnp.broadcast_to(firsts[o : o + 1, :], (tile, LANES))
            weight = jnp.take_along_axis(
                weights[o, :, pl.ds(at, LANES)].astype(F32), (sublane - first) & (tile - 1), axis=0
            )
            group = ((first - sublane + (tile - 1)) >> 3).astype(F32)
            row = 2 * o * tile
            moves[j, row : row + 2 * tile, :] = jnp.concatenate([weight, group], axis=0).astype(BF16)
        return carry

    lax.fori_loop(0, samples // LANES, offset_bands, 0)


def stack_kernel(
    arrived,
    filters_hbm,
    moves_hbm,
    centre,
    right,
    left,
    filters,
    moves,
    binned,
    ends,
    dipped,
    sems,
):
    slots = arrived.shape[0]
    half = arrived.shape[1] - LANES
    width = 2 * LANES
    pieces = [(filters_hbm.at[: filters.shape[0]], filters), (moves_hbm, moves)]
    copies = [
        pltpu.make_async_copy(source, target, sems.at[i])
        for i, (source, target) in enumerate(pieces)
    ]
    for copy in copies:
        copy.start()
    blocks = moves.shape[0]
    offsets = moves.shape[1] // 16
    lines = IL_DEV * offsets
    cells = XL_DEV * lines
    rim = XL_DEV // 2
    out_lines = 2 * XL_DEV
    codes = apart(arrived[:, half:])[0]
    rows = codes.T
    code = jnp.where(rows[0:1] > 0.5, rows[1:2] * offsets + rows[2:3], -1.0).astype(jnp.int32)
    hit = iota((cells, slots // HALVES), 0) == code
    member = jnp.where(hit, 1.0, 0.0).astype(BF16)
    fold = jnp.dot(member, codes.astype(BF16), preferred_element_type=F32)[:, 0:1]
    scale = 1.0 / jnp.maximum(fold, 1.0)
    binned[0] = jnp.zeros((XL_DEV, lines, LANES), BF16)
    binned[blocks + 1] = jnp.zeros((XL_DEV, lines, LANES), BF16)
    ends[blocks + 1] = jnp.zeros((2, lines, LANES), BF16)
    lane = iota((lines, LANES), 1)
    for n in range(0, half, width):
        parts = apart(arrived[:, n : n + width])
        for h in range(HALVES):
            value = (
                jnp.dot(member, parts[h].astype(BF16), preferred_element_type=F32) * scale
            )
            for b in range(width // LANES):
                at = (h * half + n) // LANES + b + 1
                block = value[:, b * LANES : (b + 1) * LANES]
                binned[at] = block.astype(BF16).reshape(XL_DEV, lines, LANES)
                for g in range(2):
                    end = block[g * rim * lines : (g * rim + 1) * lines]
                    for x in range(1, rim):
                        line = block[(g * rim + x) * lines : (g * rim + x + 1) * lines]
                        end = jnp.where(lane < x * TAIL, end, pltpu.roll(line, x * TAIL, 1))
                    ends[at, g] = end.astype(BF16)

    copies.pop(0).wait()
    group = dipped.shape[0] // STEPS

    tails = (2 * rim + 2) * LANES

    def filter_group(step, carry):
        first = step * group
        for pair in range(out_lines // 2):
            low = max(0, 2 * pair - 2 * rim)
            high = min(XL_DEV, 2 * pair + 2)
            d = low - 2 * pair + 2 * rim
            lhs = [
                binned[pl.ds(first, group), x].reshape(group * lines, LANES)
                for x in range(low, high)
            ]
            rhs = [filters[d * LANES : (d + high - low) * LANES, :]]
            for g in range(2):
                if low < (g + 1) * rim and high > g * rim:
                    tail = tails + (g * rim - 2 * pair + 2 * rim + 2) * TAIL
                    lhs.append(ends[pl.ds(first + 1, group), g].reshape(group * lines, LANES))
                    rhs.append(filters[tail : tail + rim * TAIL, :])
            value = jnp.dot(
                jnp.concatenate(lhs, axis=1),
                jnp.concatenate(rhs, axis=0),
                preferred_element_type=F32,
            )
            for m in range(group):
                for i in range(IL_DEV):
                    for s in range(2):
                        line = (2 * pair + s - rim) % out_lines
                        at = m * lines + i * offsets
                        to = pl.ds(i * out_lines + line, offsets, stride=STRIDE)
                        dipped[first + m, to, :] = value[
                            at : at + offsets, s * LANES : (s + 1) * LANES
                        ]
        return carry

    lax.fori_loop(0, STEPS, filter_group, 0)
    copies.pop(0).wait()

    span = 2 * out_lines
    root = 1.0 / math.sqrt(offsets)
    tile = 8
    nothing = jnp.zeros((2 * tile, LANES), BF16)

    def move_out(j, carry):
        at = pl.multiple_of(j * LANES, LANES)
        total = jnp.zeros((span, LANES), F32)
        lhs, band = [], []
        for o in range(offsets):
            row = 2 * o * tile
            weight = moves[j, row : row + tile, :].astype(F32)
            weight = jnp.concatenate([weight, weight], axis=0).astype(BF16)
            group = moves[j, row + tile : row + 2 * tile, :].astype(F32)
            group = jnp.concatenate([group, group - 1.0], axis=0).astype(BF16)
            band += [jnp.where(group == float(g), weight, nothing) for g in range(0, 32, 2)]
            rows = pl.ds(o * STRIDE, span)
            lhs += [dipped[j, rows, :].astype(BF16), dipped[j + 1, rows, :].astype(BF16)]
            if o % MERGE == MERGE - 1:
                total = total + jnp.dot(
                    jnp.concatenate(lhs, axis=1),
                    jnp.concatenate(band, axis=0),
                    preferred_element_type=F32,
                )
                lhs, band = [], []
        total = total * root
        for i in range(IL_DEV):
            base = i * out_lines
            edge = pl.ds(i * rim, rim)
            centre[i, :, pl.ds(at, LANES)] = total[base : base + XL_DEV, :]
            right[edge, pl.ds(at, LANES)] = total[base + XL_DEV : base + XL_DEV + rim, :].astype(BF16)
            left[edge, pl.ds(at, LANES)] = total[base + XL_DEV + rim : base + out_lines, :].astype(BF16)
        return carry

    lax.fori_loop(0, blocks, move_out, 0)


def whole(count):
    return [pl.BlockSpec(memory_space=pltpu.VMEM)] * count


def send_call(traces, shot_filter, channel_gain, bin_owner, bin_slot, offset_class, owners):
    rows, samples = traces.shape
    width = samples // HALVES + LANES
    per_owner = CAP * HALVES
    return pl.pallas_call(
        send_kernel,
        out_shape=jax.ShapeDtypeStruct((owners * per_owner, width), BF16),
        in_specs=[pl.BlockSpec(memory_space=pl.ANY)] * 6,
        out_specs=pl.BlockSpec(memory_space=pl.ANY),
        scratch_shapes=[
            pltpu.VMEM(shot_filter.shape, BF16),
            pltpu.VMEM((1, rows), F32),
            pltpu.VMEM((1, rows), jnp.int32),
            pltpu.VMEM((1, rows), jnp.int32),
            pltpu.VMEM((1, rows), jnp.int32),
            pltpu.VMEM((rows, samples), BF16),
            pltpu.VMEM((owners * per_owner, width), BF16),
            pltpu.VMEM((HALVES * rows, samples // HALVES), BF16),
            pltpu.SemaphoreType.DMA((2 + samples // HALVES // (2 * LANES),)),
            pltpu.SemaphoreType.DMA((5,)),
        ],
    )(
        traces,
        shot_filter,
        channel_gain.reshape(1, rows),
        bin_owner.reshape(1, rows),
        bin_slot.reshape(1, rows),
        offset_class.reshape(1, rows),
    )


def prepare_call(dip_filter, nmo_start, nmo_weights):
    offsets, samples = nmo_start.shape
    taps_x, taps_t = dip_filter.shape
    spread = jnp.pad(dip_filter[:, ::-1].astype(F32), ((0, 0), (2 * LANES - taps_t, 0)))
    return pl.pallas_call(
        prepare_kernel,
        out_shape=(
            jax.ShapeDtypeStruct((FILTER_ROWS, 2 * LANES), BF16),
            jax.ShapeDtypeStruct((samples // LANES, offsets * 16, LANES), BF16),
        ),
        in_specs=whole(3),
        out_specs=tuple(whole(2)),
        compiler_params=pltpu.CompilerParams(vmem_limit_bytes=20 * 2**20),
    )(spread, nmo_start, nmo_weights)


def stack_call(arrived, filters, moves):
    blocks = moves.shape[0]
    offsets = moves.shape[1] // 16
    samples = blocks * LANES
    lines = IL_DEV * offsets
    edge = jax.ShapeDtypeStruct((IL_DEV * XL_DEV // 2, samples), BF16)
    return pl.pallas_call(
        stack_kernel,
        out_shape=(jax.ShapeDtypeStruct((IL_DEV, XL_DEV, samples), F32), edge, edge),
        in_specs=whole(1) + [pl.BlockSpec(memory_space=pl.ANY)] * 2,
        out_specs=tuple(whole(3)),
        scratch_shapes=[
            pltpu.VMEM(((XL_DEV + 2) * LANES + (XL_DEV + 6) * TAIL, 2 * LANES), BF16),
            pltpu.VMEM(moves.shape, BF16),
            pltpu.VMEM((blocks + 2, XL_DEV, lines, LANES), BF16),
            pltpu.VMEM((blocks + 3, 2, lines, LANES), BF16),
            pltpu.VMEM((blocks + 2, offsets * STRIDE, LANES), F32),
            pltpu.SemaphoreType.DMA((2,)),
        ],
        compiler_params=pltpu.CompilerParams(vmem_limit_bytes=49 * 2**20),
    )(arrived, filters, moves)


def per_device(
    traces,
    shot_filter,
    channel_gain,
    bin_owner,
    bin_slot,
    offset_class,
    dip_filter,
    nmo_start,
    nmo_weights,
):
    owners = lax.axis_size("shot") * lax.axis_size("bin")
    outgoing = send_call(
        traces, shot_filter, channel_gain, bin_owner, bin_slot, offset_class, owners
    )
    rows, width = outgoing.shape
    arrived = lax.all_to_all(
        outgoing.reshape(owners, rows // owners, width), ("shot", "bin"), 0, 0, tiled=True
    ).reshape(rows, width)
    prepared = prepare_call(dip_filter, nmo_start, nmo_weights)
    centre, right, left = stack_call(arrived, *prepared)
    count = lax.axis_size("bin")
    ends = range(count - 1)
    from_left = lax.ppermute(right, "bin", [(i, i + 1) for i in ends])
    from_right = lax.ppermute(left, "bin", [(i + 1, i) for i in ends])
    shape = (IL_DEV, XL_DEV // 2, centre.shape[2])
    return centre + jnp.concatenate(
        [from_left.reshape(shape), from_right.reshape(shape)], axis=1
    ).astype(F32)


def solution(mesh):
    placed = (
        P(("shot", "bin"), None),
        P(("shot", "bin"), None),
        P(),
        P(("shot", "bin"), None),
        P(("shot", "bin")),
        P(("shot", "bin")),
        P(),
        P(),
        P(),
    )
    return jax.shard_map(
        per_device, mesh=mesh, in_specs=placed, out_specs=P("shot", "bin", None), check_vma=False
    )
```

```python
import math

import jax
import jax.numpy as jnp
from jax import lax
from jax.experimental import pallas as pl
from jax.experimental.pallas import tpu as pltpu
from jax.sharding import PartitionSpec as P

LANES = 128
IL_DEV = 2
XL_DEV = 8
CAP = 4
HALVES = 2
STEPS = 2
STRIDE = 33
TAIL = 32
DIP_REACH = 15
FILTER_ROWS = 8192
MOVE_ROWS = 32
MERGE = 4
BLOCKS_AT_ONCE = 4
F32 = jnp.float32
BF16 = jnp.bfloat16


def iota(shape, dim):
    return lax.broadcasted_iota(jnp.int32, shape, dim)


def woven(first, second):
    rows, width = first.shape
    first, second = first.reshape(rows // 8, 8, width), second.reshape(rows // 8, 8, width)
    low = iota(first.shape, 1) < CAP
    even = jnp.where(low, first, pltpu.roll(second, CAP, 1))
    odd = jnp.where(low, pltpu.roll(first, CAP, 1), second)
    return jnp.stack([even, odd], axis=1).reshape(2 * rows, width)


def apart(rows):
    count, width = rows.shape
    pairs = rows.astype(F32).reshape(count // 16, 2, 8, width)
    even, odd = pairs[:, 0], pairs[:, 1]
    low = iota(even.shape, 1) < CAP
    first = jnp.where(low, even, pltpu.roll(odd, CAP, 1))
    second = jnp.where(low, pltpu.roll(even, CAP, 1), odd)
    return first.reshape(count // 2, width), second.reshape(count // 2, width)


def send_kernel(
    traces_hbm,
    shot_filter_hbm,
    gain_hbm,
    owner_hbm,
    slot_hbm,
    offset_hbm,
    out_hbm,
    shot_filter,
    gain,
    owner,
    slot,
    offset,
    traces,
    out,
    filtered,
    sems,
    small_sems,
):
    rows, samples = traces.shape
    blocks = samples // LANES
    half = samples // HALVES
    pieces = [
        (owner_hbm, owner),
        (slot_hbm, slot),
        (offset_hbm, offset),
        (gain_hbm, gain),
        (shot_filter_hbm, shot_filter),
    ]
    small = [
        pltpu.make_async_copy(source, target, small_sems.at[i])
        for i, (source, target) in enumerate(pieces)
    ]
    for copy in small:
        copy.start()
    fetch = pltpu.make_async_copy(traces_hbm, traces, sems.at[0])
    fetch.start()
    copies = []

    def send(n, stop):
        columns = (slice(None), slice(n, stop))
        copy = pltpu.make_async_copy(
            out.at[columns], out_hbm.at[columns], sems.at[1 + len(copies)]
        )
        copy.start()
        copies.append(copy)

    for copy in small:
        copy.wait()
    slots = slot[...]
    hi = (slots % XL_DEV) * IL_DEV + slots // XL_DEV
    lo = offset[...]
    lane_row = iota((LANES, rows), 0)
    table = jnp.where(lane_row == 0, 1.0, 0.0)
    table = jnp.where(lane_row == 1, jnp.broadcast_to(hi.astype(F32), table.shape), table)
    table = jnp.where(lane_row == 2, jnp.broadcast_to(lo.astype(F32), table.shape), table)
    table = jnp.where(lane_row == 3, jnp.broadcast_to(gain[...], table.shape), table)
    table = jnp.where(lane_row == 4, jnp.broadcast_to(owner[...].astype(F32), table.shape), table)
    columns = table.T
    gain_column = columns[:, 3:4]
    owner_column = columns[:, 4:5].astype(jnp.int32)
    codes = jnp.where(iota(columns.shape, 1) < 3, columns, 0.0).astype(BF16)
    owner_row = owner[...]
    same = (owner_column == owner_row) & (iota((rows, rows), 0) < iota((rows, rows), 1))
    rank = jnp.sum(jnp.where(same, 1.0, 0.0), axis=0, keepdims=True).astype(jnp.int32)
    row_ids = iota((out.shape[0] // HALVES, rows), 0)
    placed = jnp.where(row_ids == owner_row * CAP + rank, 1.0, 0.0).astype(BF16)
    taps = jnp.broadcast_to(shot_filter[...].astype(F32), (LANES, LANES))
    circulant = pltpu.roll(taps, 0, 1, stride=1, stride_axis=0)
    later = iota((LANES, LANES), 0) > iota((LANES, LANES), 1)
    before = jnp.where(later, circulant, 0.0).astype(BF16)
    centre = jnp.where(later, 0.0, circulant).astype(BF16)
    matrix = jnp.concatenate([before, centre], axis=0)
    part = jnp.dot(placed, codes, preferred_element_type=F32)
    out[:, half:] = woven(part, part).astype(BF16)
    send(half, half + LANES)
    fetch.wait()
    for j in range(blocks):
        if j == 0:
            value = jnp.dot(traces[:, :LANES], centre, preferred_element_type=F32)
        else:
            value = jnp.dot(
                traces[:, (j - 1) * LANES : (j + 1) * LANES], matrix, preferred_element_type=F32
            )
        h, at = divmod(j * LANES, half)
        filtered[h * rows : (h + 1) * rows, at : at + LANES] = (value * gain_column).astype(BF16)
    width = 2 * LANES
    for n in range(0, half, width):
        parts = [
            jnp.dot(
                placed,
                filtered[h * rows : (h + 1) * rows, n : n + width],
                preferred_element_type=F32,
            )
            for h in range(HALVES)
        ]
        out[:, n : n + width] = woven(*parts).astype(BF16)
        send(n, n + width)
    for copy in copies:
        copy.wait()


def prepare_kernel(dip, start, weights, filters, moves):
    taps_x = dip.shape[0]
    offsets, samples = start.shape
    bands = []
    for a in range(taps_x):
        spread = jnp.broadcast_to(dip[a : a + 1, :], (LANES + TAIL, 2 * LANES))
        bands.append(pltpu.roll(spread, 1, 1, stride=1, stride_axis=0)[:, :LANES].astype(BF16))
    none = jnp.zeros((LANES + TAIL, LANES), BF16)
    for d in range(-2, taps_x + 3):
        pair = [bands[a] if 0 <= a < taps_x else none for a in (d, d - 1)]
        for s in range(2):
            lanes = slice(s * LANES, (s + 1) * LANES)
            if 0 <= d <= taps_x:
                filters[d * LANES : (d + 1) * LANES, lanes] = pair[s][:LANES]
            tail = (taps_x + 1) * LANES + (d + 2) * TAIL
            filters[tail : tail + TAIL, lanes] = pair[s][LANES:]
    tile = 8
    sublane = iota((tile, LANES), 0)

    def offset_bands(j, carry):
        at = pl.multiple_of(j * LANES, LANES)
        firsts = start[:, pl.ds(at, LANES)] + (LANES - DIP_REACH - at)
        for o in range(offsets):
            first = jnp.broadcast_to(firsts[o : o + 1, :], (tile, LANES))
            weight = jnp.take_along_axis(
                weights[o, :, pl.ds(at, LANES)].astype(F32), (sublane - first) & (tile - 1), axis=0
            )
            group = ((first - sublane + (tile - 1)) >> 3).astype(F32)
            row = 2 * o * tile
            moves[j, row : row + 2 * tile, :] = jnp.concatenate([weight, group], axis=0).astype(BF16)
        return carry

    lax.fori_loop(0, samples // LANES, offset_bands, 0)


def stack_kernel(
    arrived,
    filters_hbm,
    moves_hbm,
    centre,
    right,
    left,
    filters,
    moves,
    binned,
    ends,
    dipped,
    sems,
):
    slots = arrived.shape[0]
    half = arrived.shape[1] - LANES
    width = 2 * LANES
    pieces = [
        (filters_hbm.at[: filters.shape[0]], filters),
        (moves_hbm.at[:, : moves.shape[1]], moves),
    ]
    copies = [
        pltpu.make_async_copy(source, target, sems.at[i])
        for i, (source, target) in enumerate(pieces)
    ]
    for copy in copies:
        copy.start()
    blocks = moves.shape[0]
    offsets = moves.shape[1] // 16
    lines = IL_DEV * offsets
    cells = XL_DEV * lines
    rim = XL_DEV // 2
    out_lines = 2 * XL_DEV
    codes = apart(arrived[:, half:])[0]
    rows = codes.T
    code = jnp.where(rows[0:1] > 0.5, rows[1:2] * offsets + rows[2:3], -1.0).astype(jnp.int32)
    hit = iota((cells, slots // HALVES), 0) == code
    member = jnp.where(hit, 1.0, 0.0).astype(BF16)
    fold = jnp.dot(member, codes.astype(BF16), preferred_element_type=F32)[:, 0:1]
    scale = 1.0 / jnp.maximum(fold, 1.0)
    binned[0] = jnp.zeros((XL_DEV, lines, LANES), BF16)
    binned[blocks + 1] = jnp.zeros((XL_DEV, lines, LANES), BF16)
    ends[blocks + 1] = jnp.zeros((2, lines, LANES), BF16)
    lane = iota((lines, LANES), 1)
    for n in range(0, half, width):
        parts = apart(arrived[:, n : n + width])
        for h in range(HALVES):
            value = (
                jnp.dot(member, parts[h].astype(BF16), preferred_element_type=F32) * scale
            )
            for b in range(width // LANES):
                at = (h * half + n) // LANES + b + 1
                block = value[:, b * LANES : (b + 1) * LANES]
                binned[at] = block.astype(BF16).reshape(XL_DEV, lines, LANES)
                for g in range(2):
                    end = block[g * rim * lines : (g * rim + 1) * lines]
                    for x in range(1, rim):
                        line = block[(g * rim + x) * lines : (g * rim + x + 1) * lines]
                        end = jnp.where(lane < x * TAIL, end, pltpu.roll(line, x * TAIL, 1))
                    ends[at, g] = end.astype(BF16)

    copies.pop(0).wait()
    group = dipped.shape[0] // STEPS

    tails = (2 * rim + 2) * LANES

    def filter_group(step, carry):
        first = step * group
        for pair in range(out_lines // 2):
            low = max(0, 2 * pair - 2 * rim)
            high = min(XL_DEV, 2 * pair + 2)
            d = low - 2 * pair + 2 * rim
            lhs = [
                binned[pl.ds(first, group), x].reshape(group * lines, LANES)
                for x in range(low, high)
            ]
            rhs = [filters[d * LANES : (d + high - low) * LANES, :]]
            for g in range(2):
                if low < (g + 1) * rim and high > g * rim:
                    tail = tails + (g * rim - 2 * pair + 2 * rim + 2) * TAIL
                    lhs.append(ends[pl.ds(first + 1, group), g].reshape(group * lines, LANES))
                    rhs.append(filters[tail : tail + rim * TAIL, :])
            value = jnp.dot(
                jnp.concatenate(lhs, axis=1),
                jnp.concatenate(rhs, axis=0),
                preferred_element_type=F32,
            )
            for m in range(group):
                for i in range(IL_DEV):
                    for s in range(2):
                        line = (2 * pair + s - rim) % out_lines
                        at = m * lines + i * offsets
                        to = pl.ds(i * out_lines + line, offsets, stride=STRIDE)
                        dipped[first + m, to, :] = value[
                            at : at + offsets, s * LANES : (s + 1) * LANES
                        ]
        return carry

    lax.fori_loop(0, STEPS, filter_group, 0)
    copies.pop(0).wait()

    span = 2 * out_lines
    root = 1.0 / math.sqrt(offsets)
    tile = 8
    nothing = jnp.zeros((2 * tile, LANES), BF16)

    def move_out(step, carry):
        for j in range(BLOCKS_AT_ONCE):
            move_block(step * BLOCKS_AT_ONCE + j)
        return carry

    def move_block(j):
        at = pl.multiple_of(j * LANES, LANES)
        total = jnp.zeros((span, LANES), F32)
        lhs, band = [], []
        for o in range(offsets):
            row = 2 * o * tile
            weight = moves[j, row : row + tile, :].astype(F32)
            weight = jnp.concatenate([weight, weight], axis=0).astype(BF16)
            group = moves[j, row + tile : row + 2 * tile, :].astype(F32)
            group = jnp.concatenate([group, group - 1.0], axis=0).astype(BF16)
            band += [jnp.where(group == float(g), weight, nothing) for g in range(0, 32, 2)]
            rows = pl.ds(o * STRIDE, span)
            lhs += [dipped[j, rows, :].astype(BF16), dipped[j + 1, rows, :].astype(BF16)]
            if o % MERGE == MERGE - 1:
                total = total + jnp.dot(
                    jnp.concatenate(lhs, axis=1),
                    jnp.concatenate(band, axis=0),
                    preferred_element_type=F32,
                )
                lhs, band = [], []
        total = total * root
        for i in range(IL_DEV):
            base = i * out_lines
            edge = pl.ds(i * rim, rim)
            centre[i, :, pl.ds(at, LANES)] = total[base : base + XL_DEV, :]
            right[edge, pl.ds(at, LANES)] = total[base + XL_DEV : base + XL_DEV + rim, :].astype(BF16)
            left[edge, pl.ds(at, LANES)] = total[base + XL_DEV + rim : base + out_lines, :].astype(BF16)

    lax.fori_loop(0, blocks // BLOCKS_AT_ONCE, move_out, 0)


def whole(count):
    return [pl.BlockSpec(memory_space=pltpu.VMEM)] * count


def send_call(traces, shot_filter, channel_gain, bin_owner, bin_slot, offset_class, owners):
    rows, samples = traces.shape
    width = samples // HALVES + LANES
    per_owner = CAP * HALVES
    return pl.pallas_call(
        send_kernel,
        out_shape=jax.ShapeDtypeStruct((owners * per_owner, width), BF16),
        in_specs=[pl.BlockSpec(memory_space=pl.ANY)] * 6,
        out_specs=pl.BlockSpec(memory_space=pl.ANY),
        scratch_shapes=[
            pltpu.VMEM(shot_filter.shape, BF16),
            pltpu.VMEM((1, rows), F32),
            pltpu.VMEM((1, rows), jnp.int32),
            pltpu.VMEM((1, rows), jnp.int32),
            pltpu.VMEM((1, rows), jnp.int32),
            pltpu.VMEM((rows, samples), BF16),
            pltpu.VMEM((owners * per_owner, width), BF16),
            pltpu.VMEM((HALVES * rows, samples // HALVES), BF16),
            pltpu.SemaphoreType.DMA((2 + samples // HALVES // (2 * LANES),)),
            pltpu.SemaphoreType.DMA((5,)),
        ],
    )(
        traces,
        shot_filter,
        channel_gain.reshape(1, rows),
        bin_owner.reshape(1, rows),
        bin_slot.reshape(1, rows),
        offset_class.reshape(1, rows),
    )


def prepare_call(dip_filter, nmo_start, nmo_weights):
    offsets, samples = nmo_start.shape
    taps_x, taps_t = dip_filter.shape
    spread = jnp.pad(dip_filter[:, ::-1].astype(F32), ((0, 0), (2 * LANES - taps_t, 0)))
    return pl.pallas_call(
        prepare_kernel,
        out_shape=(
            jax.ShapeDtypeStruct((FILTER_ROWS, 2 * LANES), BF16),
            jax.ShapeDtypeStruct((samples // LANES, offsets * MOVE_ROWS, LANES), BF16),
        ),
        in_specs=whole(3),
        out_specs=tuple(whole(2)),
        compiler_params=pltpu.CompilerParams(vmem_limit_bytes=20 * 2**20),
    )(spread, nmo_start, nmo_weights)


def stack_call(arrived, filters, moves):
    blocks = moves.shape[0]
    offsets = moves.shape[1] // MOVE_ROWS
    samples = blocks * LANES
    lines = IL_DEV * offsets
    edge = jax.ShapeDtypeStruct((IL_DEV * XL_DEV // 2, samples), BF16)
    return pl.pallas_call(
        stack_kernel,
        out_shape=(jax.ShapeDtypeStruct((IL_DEV, XL_DEV, samples), F32), edge, edge),
        in_specs=whole(1) + [pl.BlockSpec(memory_space=pl.ANY)] * 2,
        out_specs=tuple(whole(3)),
        scratch_shapes=[
            pltpu.VMEM(((XL_DEV + 2) * LANES + (XL_DEV + 6) * TAIL, 2 * LANES), BF16),
            pltpu.VMEM((blocks, offsets * 16, LANES), BF16),
            pltpu.VMEM((blocks + 2, XL_DEV, lines, LANES), BF16),
            pltpu.VMEM((blocks + 3, 2, lines, LANES), BF16),
            pltpu.VMEM((blocks + 2, offsets * STRIDE, LANES), F32),
            pltpu.SemaphoreType.DMA((2,)),
        ],
        compiler_params=pltpu.CompilerParams(
            vmem_limit_bytes=49 * 2**20
        ),
    )(arrived, filters, moves)


def per_device(
    traces,
    shot_filter,
    channel_gain,
    bin_owner,
    bin_slot,
    offset_class,
    dip_filter,
    nmo_start,
    nmo_weights,
):
    owners = lax.axis_size("shot") * lax.axis_size("bin")
    outgoing = send_call(
        traces, shot_filter, channel_gain, bin_owner, bin_slot, offset_class, owners
    )
    rows, width = outgoing.shape
    arrived = lax.all_to_all(
        outgoing.reshape(owners, rows // owners, width), ("shot", "bin"), 0, 0, tiled=True
    ).reshape(rows, width)
    prepared = prepare_call(dip_filter, nmo_start, nmo_weights)
    centre, right, left = stack_call(arrived, *prepared)
    count = lax.axis_size("bin")
    ends = range(count - 1)
    from_left = lax.ppermute(right, "bin", [(i, i + 1) for i in ends])
    from_right = lax.ppermute(left, "bin", [(i + 1, i) for i in ends])
    shape = (IL_DEV, XL_DEV // 2, centre.shape[2])
    return centre + jnp.concatenate(
        [from_left.reshape(shape), from_right.reshape(shape)], axis=1
    ).astype(F32)


def solution(mesh):
    placed = (
        P(("shot", "bin"), None),
        P(("shot", "bin"), None),
        P(),
        P(("shot", "bin"), None),
        P(("shot", "bin")),
        P(("shot", "bin")),
        P(),
        P(),
        P(),
    )
    return jax.shard_map(
        per_device, mesh=mesh, in_specs=placed, out_specs=P("shot", "bin", None), check_vma=False
    )
```

```python
import math

import jax
import jax.numpy as jnp
from jax import lax
from jax.experimental import pallas as pl
from jax.experimental.pallas import tpu as pltpu
from jax.sharding import PartitionSpec as P

LANES = 128
IL_DEV = 2
XL_DEV = 8
CAP = 4
HALVES = 2
STEPS = 2
STRIDE = 33
TAIL = 32
DIP_REACH = 15
FILTER_ROWS = 8192
MOVE_ROWS = 32
MERGE = 4
BLOCKS_AT_ONCE = 8
F32 = jnp.float32
BF16 = jnp.bfloat16


def iota(shape, dim):
    return lax.broadcasted_iota(jnp.int32, shape, dim)


def woven(first, second):
    rows, width = first.shape
    first, second = first.reshape(rows // 8, 8, width), second.reshape(rows // 8, 8, width)
    low = iota(first.shape, 1) < CAP
    even = jnp.where(low, first, pltpu.roll(second, CAP, 1))
    odd = jnp.where(low, pltpu.roll(first, CAP, 1), second)
    return jnp.stack([even, odd], axis=1).reshape(2 * rows, width)


def apart(rows):
    count, width = rows.shape
    pairs = rows.astype(F32).reshape(count // 16, 2, 8, width)
    even, odd = pairs[:, 0], pairs[:, 1]
    low = iota(even.shape, 1) < CAP
    first = jnp.where(low, even, pltpu.roll(odd, CAP, 1))
    second = jnp.where(low, pltpu.roll(even, CAP, 1), odd)
    return first.reshape(count // 2, width), second.reshape(count // 2, width)


def send_kernel(
    traces_hbm,
    shot_filter_hbm,
    gain_hbm,
    owner_hbm,
    slot_hbm,
    offset_hbm,
    out_hbm,
    shot_filter,
    gain,
    owner,
    slot,
    offset,
    traces,
    out,
    filtered,
    sems,
    small_sems,
):
    rows, samples = traces.shape
    blocks = samples // LANES
    half = samples // HALVES
    pieces = [
        (owner_hbm, owner),
        (slot_hbm, slot),
        (offset_hbm, offset),
        (gain_hbm, gain),
        (shot_filter_hbm, shot_filter),
    ]
    small = [
        pltpu.make_async_copy(source, target, small_sems.at[i])
        for i, (source, target) in enumerate(pieces)
    ]
    for copy in small:
        copy.start()
    fetch = pltpu.make_async_copy(traces_hbm, traces, sems.at[0])
    fetch.start()
    copies = []

    def send(n, stop):
        columns = (slice(None), slice(n, stop))
        copy = pltpu.make_async_copy(
            out.at[columns], out_hbm.at[columns], sems.at[1 + len(copies)]
        )
        copy.start()
        copies.append(copy)

    for copy in small:
        copy.wait()
    slots = slot[...]
    hi = (slots % XL_DEV) * IL_DEV + slots // XL_DEV
    lo = offset[...]
    lane_row = iota((LANES, rows), 0)
    table = jnp.where(lane_row == 0, 1.0, 0.0)
    table = jnp.where(lane_row == 1, jnp.broadcast_to(hi.astype(F32), table.shape), table)
    table = jnp.where(lane_row == 2, jnp.broadcast_to(lo.astype(F32), table.shape), table)
    table = jnp.where(lane_row == 3, jnp.broadcast_to(gain[...], table.shape), table)
    table = jnp.where(lane_row == 4, jnp.broadcast_to(owner[...].astype(F32), table.shape), table)
    columns = table.T
    gain_column = columns[:, 3:4]
    owner_column = columns[:, 4:5].astype(jnp.int32)
    codes = jnp.where(iota(columns.shape, 1) < 3, columns, 0.0).astype(BF16)
    owner_row = owner[...]
    same = (owner_column == owner_row) & (iota((rows, rows), 0) < iota((rows, rows), 1))
    rank = jnp.sum(jnp.where(same, 1.0, 0.0), axis=0, keepdims=True).astype(jnp.int32)
    row_ids = iota((out.shape[0] // HALVES, rows), 0)
    placed = jnp.where(row_ids == owner_row * CAP + rank, 1.0, 0.0).astype(BF16)
    taps = jnp.broadcast_to(shot_filter[...].astype(F32), (LANES, LANES))
    circulant = pltpu.roll(taps, 0, 1, stride=1, stride_axis=0)
    later = iota((LANES, LANES), 0) > iota((LANES, LANES), 1)
    before = jnp.where(later, circulant, 0.0).astype(BF16)
    centre = jnp.where(later, 0.0, circulant).astype(BF16)
    matrix = jnp.concatenate([before, centre], axis=0)
    part = jnp.dot(placed, codes, preferred_element_type=F32)
    out[:, half:] = woven(part, part).astype(BF16)
    send(half, half + LANES)
    fetch.wait()
    for j in range(blocks):
        if j == 0:
            value = jnp.dot(traces[:, :LANES], centre, preferred_element_type=F32)
        else:
            value = jnp.dot(
                traces[:, (j - 1) * LANES : (j + 1) * LANES], matrix, preferred_element_type=F32
            )
        h, at = divmod(j * LANES, half)
        filtered[h * rows : (h + 1) * rows, at : at + LANES] = (value * gain_column).astype(BF16)
    width = 2 * LANES
    for n in range(0, half, width):
        parts = [
            jnp.dot(
                placed,
                filtered[h * rows : (h + 1) * rows, n : n + width],
                preferred_element_type=F32,
            )
            for h in range(HALVES)
        ]
        out[:, n : n + width] = woven(*parts).astype(BF16)
        send(n, n + width)
    for copy in copies:
        copy.wait()


def prepare_kernel(dip, start, weights, filters, moves):
    taps_x = dip.shape[0]
    offsets, samples = start.shape
    bands = []
    for a in range(taps_x):
        spread = jnp.broadcast_to(dip[a : a + 1, :], (LANES + TAIL, 2 * LANES))
        bands.append(pltpu.roll(spread, 1, 1, stride=1, stride_axis=0)[:, :LANES].astype(BF16))
    none = jnp.zeros((LANES + TAIL, LANES), BF16)
    for d in range(-2, taps_x + 3):
        pair = [bands[a] if 0 <= a < taps_x else none for a in (d, d - 1)]
        for s in range(2):
            lanes = slice(s * LANES, (s + 1) * LANES)
            if 0 <= d <= taps_x:
                filters[d * LANES : (d + 1) * LANES, lanes] = pair[s][:LANES]
            tail = (taps_x + 1) * LANES + (d + 2) * TAIL
            filters[tail : tail + TAIL, lanes] = pair[s][LANES:]
    tile = 8
    sublane = iota((tile, LANES), 0)

    def offset_bands(j, carry):
        at = pl.multiple_of(j * LANES, LANES)
        firsts = start[:, pl.ds(at, LANES)] + (LANES - DIP_REACH - at)
        for o in range(offsets):
            first = jnp.broadcast_to(firsts[o : o + 1, :], (tile, LANES))
            weight = jnp.take_along_axis(
                weights[o, :, pl.ds(at, LANES)].astype(F32), (sublane - first) & (tile - 1), axis=0
            )
            group = ((first - sublane + (tile - 1)) >> 3).astype(F32)
            row = 2 * o * tile
            moves[j, row : row + 2 * tile, :] = jnp.concatenate([weight, group], axis=0).astype(BF16)
        return carry

    lax.fori_loop(0, samples // LANES, offset_bands, 0)


def stack_kernel(
    arrived,
    filters_hbm,
    moves_hbm,
    centre,
    right,
    left,
    filters,
    moves,
    binned,
    ends,
    dipped,
    sems,
):
    slots = arrived.shape[0]
    half = arrived.shape[1] - LANES
    width = 2 * LANES
    pieces = [
        (filters_hbm.at[: filters.shape[0]], filters),
        (moves_hbm.at[:, : moves.shape[1]], moves),
    ]
    copies = [
        pltpu.make_async_copy(source, target, sems.at[i])
        for i, (source, target) in enumerate(pieces)
    ]
    for copy in copies:
        copy.start()
    blocks = moves.shape[0]
    offsets = moves.shape[1] // 16
    lines = IL_DEV * offsets
    cells = XL_DEV * lines
    rim = XL_DEV // 2
    out_lines = 2 * XL_DEV
    codes = apart(arrived[:, half:])[0]
    rows = codes.T
    code = jnp.where(rows[0:1] > 0.5, rows[1:2] * offsets + rows[2:3], -1.0).astype(jnp.int32)
    hit = iota((cells, slots // HALVES), 0) == code
    member = jnp.where(hit, 1.0, 0.0).astype(BF16)
    fold = jnp.dot(member, codes.astype(BF16), preferred_element_type=F32)[:, 0:1]
    scale = 1.0 / jnp.maximum(fold, 1.0)
    binned[0] = jnp.zeros((XL_DEV, lines, LANES), BF16)
    binned[blocks + 1] = jnp.zeros((XL_DEV, lines, LANES), BF16)
    ends[blocks + 1] = jnp.zeros((2, lines, LANES), BF16)
    lane = iota((lines, LANES), 1)
    for n in range(0, half, width):
        parts = apart(arrived[:, n : n + width])
        for h in range(HALVES):
            value = (
                jnp.dot(member, parts[h].astype(BF16), preferred_element_type=F32) * scale
            )
            for b in range(width // LANES):
                at = (h * half + n) // LANES + b + 1
                block = value[:, b * LANES : (b + 1) * LANES]
                binned[at] = block.astype(BF16).reshape(XL_DEV, lines, LANES)
                for g in range(2):
                    end = block[g * rim * lines : (g * rim + 1) * lines]
                    for x in range(1, rim):
                        line = block[(g * rim + x) * lines : (g * rim + x + 1) * lines]
                        end = jnp.where(lane < x * TAIL, end, pltpu.roll(line, x * TAIL, 1))
                    ends[at, g] = end.astype(BF16)

    copies.pop(0).wait()
    group = dipped.shape[0] // STEPS

    tails = (2 * rim + 2) * LANES

    def filter_group(step, carry):
        first = step * group
        for pair in range(out_lines // 2):
            low = max(0, 2 * pair - 2 * rim)
            high = min(XL_DEV, 2 * pair + 2)
            d = low - 2 * pair + 2 * rim
            lhs = [
                binned[pl.ds(first, group), x].reshape(group * lines, LANES)
                for x in range(low, high)
            ]
            rhs = [filters[d * LANES : (d + high - low) * LANES, :]]
            for g in range(2):
                if low < (g + 1) * rim and high > g * rim:
                    tail = tails + (g * rim - 2 * pair + 2 * rim + 2) * TAIL
                    lhs.append(ends[pl.ds(first + 1, group), g].reshape(group * lines, LANES))
                    rhs.append(filters[tail : tail + rim * TAIL, :])
            value = jnp.dot(
                jnp.concatenate(lhs, axis=1),
                jnp.concatenate(rhs, axis=0),
                preferred_element_type=F32,
            )
            for m in range(group):
                for i in range(IL_DEV):
                    for s in range(2):
                        line = (2 * pair + s - rim) % out_lines
                        at = m * lines + i * offsets
                        to = pl.ds(i * out_lines + line, offsets, stride=STRIDE)
                        dipped[first + m, to, :] = value[
                            at : at + offsets, s * LANES : (s + 1) * LANES
                        ]
        return carry

    lax.fori_loop(0, STEPS, filter_group, 0)
    copies.pop(0).wait()

    span = 2 * out_lines
    root = 1.0 / math.sqrt(offsets)
    tile = 8
    nothing = jnp.zeros((2 * tile, LANES), BF16)

    def move_out(step, carry):
        for j in range(BLOCKS_AT_ONCE):
            move_block(step * BLOCKS_AT_ONCE + j)
        return carry

    def move_block(j):
        at = pl.multiple_of(j * LANES, LANES)
        total = jnp.zeros((span, LANES), F32)
        lhs, band = [], []
        for o in range(offsets):
            row = 2 * o * tile
            weight = moves[j, row : row + tile, :].astype(F32)
            weight = jnp.concatenate([weight, weight], axis=0).astype(BF16)
            group = moves[j, row + tile : row + 2 * tile, :].astype(F32)
            group = jnp.concatenate([group, group - 1.0], axis=0).astype(BF16)
            band += [jnp.where(group == float(g), weight, nothing) for g in range(0, 32, 2)]
            rows = pl.ds(o * STRIDE, span)
            lhs += [dipped[j, rows, :].astype(BF16), dipped[j + 1, rows, :].astype(BF16)]
            if o % MERGE == MERGE - 1:
                total = total + jnp.dot(
                    jnp.concatenate(lhs, axis=1),
                    jnp.concatenate(band, axis=0),
                    preferred_element_type=F32,
                )
                lhs, band = [], []
        total = total * root
        for i in range(IL_DEV):
            base = i * out_lines
            edge = pl.ds(i * rim, rim)
            centre[i, :, pl.ds(at, LANES)] = total[base : base + XL_DEV, :]
            right[edge, pl.ds(at, LANES)] = total[base + XL_DEV : base + XL_DEV + rim, :].astype(BF16)
            left[edge, pl.ds(at, LANES)] = total[base + XL_DEV + rim : base + out_lines, :].astype(BF16)

    lax.fori_loop(0, blocks // BLOCKS_AT_ONCE, move_out, 0)


def whole(count):
    return [pl.BlockSpec(memory_space=pltpu.VMEM)] * count


def send_call(traces, shot_filter, channel_gain, bin_owner, bin_slot, offset_class, owners):
    rows, samples = traces.shape
    width = samples // HALVES + LANES
    per_owner = CAP * HALVES
    return pl.pallas_call(
        send_kernel,
        out_shape=jax.ShapeDtypeStruct((owners * per_owner, width), BF16),
        in_specs=[pl.BlockSpec(memory_space=pl.ANY)] * 6,
        out_specs=pl.BlockSpec(memory_space=pl.ANY),
        scratch_shapes=[
            pltpu.VMEM(shot_filter.shape, BF16),
            pltpu.VMEM((1, rows), F32),
            pltpu.VMEM((1, rows), jnp.int32),
            pltpu.VMEM((1, rows), jnp.int32),
            pltpu.VMEM((1, rows), jnp.int32),
            pltpu.VMEM((rows, samples), BF16),
            pltpu.VMEM((owners * per_owner, width), BF16),
            pltpu.VMEM((HALVES * rows, samples // HALVES), BF16),
            pltpu.SemaphoreType.DMA((2 + samples // HALVES // (2 * LANES),)),
            pltpu.SemaphoreType.DMA((5,)),
        ],
    )(
        traces,
        shot_filter,
        channel_gain.reshape(1, rows),
        bin_owner.reshape(1, rows),
        bin_slot.reshape(1, rows),
        offset_class.reshape(1, rows),
    )


def prepare_call(dip_filter, nmo_start, nmo_weights):
    offsets, samples = nmo_start.shape
    taps_x, taps_t = dip_filter.shape
    spread = jnp.pad(dip_filter[:, ::-1].astype(F32), ((0, 0), (2 * LANES - taps_t, 0)))
    return pl.pallas_call(
        prepare_kernel,
        out_shape=(
            jax.ShapeDtypeStruct((FILTER_ROWS, 2 * LANES), BF16),
            jax.ShapeDtypeStruct((samples // LANES, offsets * MOVE_ROWS, LANES), BF16),
        ),
        in_specs=whole(3),
        out_specs=tuple(whole(2)),
        compiler_params=pltpu.CompilerParams(vmem_limit_bytes=20 * 2**20),
    )(spread, nmo_start, nmo_weights)


def stack_call(arrived, filters, moves):
    blocks = moves.shape[0]
    offsets = moves.shape[1] // MOVE_ROWS
    samples = blocks * LANES
    lines = IL_DEV * offsets
    edge = jax.ShapeDtypeStruct((IL_DEV * XL_DEV // 2, samples), BF16)
    return pl.pallas_call(
        stack_kernel,
        out_shape=(jax.ShapeDtypeStruct((IL_DEV, XL_DEV, samples), F32), edge, edge),
        in_specs=whole(1) + [pl.BlockSpec(memory_space=pl.ANY)] * 2,
        out_specs=tuple(whole(3)),
        scratch_shapes=[
            pltpu.VMEM(((XL_DEV + 2) * LANES + (XL_DEV + 6) * TAIL, 2 * LANES), BF16),
            pltpu.VMEM((blocks, offsets * 16, LANES), BF16),
            pltpu.VMEM((blocks + 2, XL_DEV, lines, LANES), BF16),
            pltpu.VMEM((blocks + 3, 2, lines, LANES), BF16),
            pltpu.VMEM((blocks + 2, offsets * STRIDE, LANES), F32),
            pltpu.SemaphoreType.DMA((2,)),
        ],
        compiler_params=pltpu.CompilerParams(
            vmem_limit_bytes=49 * 2**20
        ),
    )(arrived, filters, moves)


def per_device(
    traces,
    shot_filter,
    channel_gain,
    bin_owner,
    bin_slot,
    offset_class,
    dip_filter,
    nmo_start,
    nmo_weights,
):
    owners = lax.axis_size("shot") * lax.axis_size("bin")
    outgoing = send_call(
        traces, shot_filter, channel_gain, bin_owner, bin_slot, offset_class, owners
    )
    rows, width = outgoing.shape
    arrived = lax.all_to_all(
        outgoing.reshape(owners, rows // owners, width), ("shot", "bin"), 0, 0, tiled=True
    ).reshape(rows, width)
    prepared = prepare_call(dip_filter, nmo_start, nmo_weights)
    centre, right, left = stack_call(arrived, *prepared)
    count = lax.axis_size("bin")
    ends = range(count - 1)
    from_left = lax.ppermute(right, "bin", [(i, i + 1) for i in ends])
    from_right = lax.ppermute(left, "bin", [(i + 1, i) for i in ends])
    shape = (IL_DEV, XL_DEV // 2, centre.shape[2])
    return centre + jnp.concatenate(
        [from_left.reshape(shape), from_right.reshape(shape)], axis=1
    ).astype(F32)


def solution(mesh):
    placed = (
        P(("shot", "bin"), None),
        P(("shot", "bin"), None),
        P(),
        P(("shot", "bin"), None),
        P(("shot", "bin")),
        P(("shot", "bin")),
        P(),
        P(),
        P(),
    )
    return jax.shard_map(
        per_device, mesh=mesh, in_specs=placed, out_specs=P("shot", "bin", None), check_vma=False
    )
```
